32 devices in a mesh: wide: 8 (over z, y), narrow: 4 (over x, core).
Axes of the slice: x: 2, y: 2, z: 4, core: 2. Of those that a mesh axis runs over, the one named last changes fastest.
Arguments:
- amplitudes: float32 [8, 512, 1024], P('wide', None, 'narrow'), may hold values from -6 to 6
- partner: float32 [64, 2048, 1024], P(None, 'wide', 'narrow'), may hold values from -0.1875 to 0.1875
- gate_block: float32 [8, 8], replicated, may hold values from -2 to 2
- slice_bits: int32 [6], replicated, may hold values from 0 to 1, as said below
- bit_order: int32 [9], replicated, may hold values from 0 to 8, each once
Outputs:
- contracted: float32 [8, 512, 2048], P(None, 'wide', 'narrow')
The draws below stay inside these ranges and needn't reach their ends.
Inputs may be any that keep to these rules, and one draw needn't show every extreme that they name: bit_order is a permutation of 0 to 8. `slice_bits`: each entry is 0 or 1; the bits are never all equal.
All inputs are finite; a program needn't handle non-finite values.
Results may differ from the reference program's by a relative error of at most 0.00007.
Values sent between devices are 32-bit elements; how exact they have to be, the bound alone decides.
A program may use at most 64 MiB of HBM per device.

```python
import jax
import jax.numpy as jnp
from jax import lax

LBITS = 9
ML = 512
MH = 8
Q = 8
K = 1024
N = 2048
SBITS = 6
S = 64


def draw_slice_bits(key, part):
    number = jax.random.randint(key, (), 1, S - 1, dtype=jnp.int32)
    shifts = jnp.arange(SBITS, dtype=jnp.int32)
    return jnp.bitwise_and(jnp.right_shift(number, shifts), 1).astype(jnp.int32)


def level_of(key, dims, split, smallest, high):
    factor_of = 1.0
    for axis_at, shards_of in split:
        steps = jax.random.uniform(jax.random.fold_in(jax.random.fold_in(key, 6), axis_at), (shards_of,), jnp.float32, smallest / len(split), high / len(split))
        factor_of = factor_of * jnp.repeat(jnp.exp(steps), dims[axis_at] // shards_of).reshape((-1,) + (1,) * (len(dims) - 1 - axis_at))
    return factor_of


def centred(own_key, extent, deviation, reach, pieces=(), kind=jnp.bfloat16):
    loudness = level_of(own_key, extent, pieces, -0.22, 0.18) if pieces else 1.0
    array = jax.random.normal(own_key, extent, jnp.float32) * deviation * loudness
    return jnp.minimum(jnp.maximum(array, -reach), reach).astype(kind)


def setup_inputs(seed: int = 0) -> dict:
    arg_keys = jax.random.split(jax.random.key(seed), 6)
    return {
        "amplitudes": centred(arg_keys[0], (MH, ML, K), 1.0, 6.0, ((0, 8), (2, 4)), jnp.float32),
        "partner": centred(arg_keys[1], (S, N, K), K ** -0.5, 0.1875, ((1, 8), (2, 4)), jnp.float32),
        "gate_block": centred(arg_keys[2], (Q, MH), MH ** -0.5, 2.0, (), jnp.float32),
        "slice_bits": draw_slice_bits(jax.random.fold_in(arg_keys[5], 71), 0),
        "bit_order": jax.random.permutation(arg_keys[4], LBITS).astype(jnp.int32),
    }


def source_rows(bit_order, total_rows):
    width = bit_order.shape[0]
    row_ids = jnp.arange(total_rows, dtype=jnp.int32)
    picked = jnp.bitwise_and(jnp.right_shift(row_ids[:, None], bit_order[None, :].astype(jnp.int32)), 1)
    powers = jnp.left_shift(jnp.ones((width,), jnp.int32), jnp.arange(width, dtype=jnp.int32))
    return jnp.sum(picked * powers[None, :], axis=1).astype(jnp.int32)


def slice_number(slice_bits):
    width = slice_bits.shape[0]
    powers = jnp.left_shift(jnp.ones((width,), jnp.int32), jnp.arange(width, dtype=jnp.int32))
    return jnp.sum(slice_bits.astype(jnp.int32) * powers).astype(jnp.int32)


def reference(amplitudes, partner, gate_block, slice_bits, bit_order):
    source = source_rows(bit_order, amplitudes.shape[1])
    reordered = jnp.take(amplitudes, source, axis=1)
    chosen = lax.dynamic_index_in_dim(partner, slice_number(slice_bits), 0, keepdims=False)
    joined = jnp.einsum('hlk,nk->hln', reordered, chosen, precision=lax.Precision.HIGHEST)
    return jnp.einsum('qh,hln->qln', gate_block, joined, precision=lax.Precision.HIGHEST)
```

```python
import functools

import jax
import jax.numpy as jnp
from jax import lax
from jax.experimental import pallas as pl
from jax.experimental.pallas import tpu as pltpu
from jax.sharding import PartitionSpec as P

F32 = jnp.float32
BF16 = jnp.bfloat16
MESH = pl.DeviceIdType.MESH


def slice_kernel(bits_ref, partner_ref, chosen_ref, sem):
    number = bits_ref[0]
    for j in range(1, bits_ref.shape[0]):
        number = number + bits_ref[j] * (1 << j)
    copy = pltpu.make_async_copy(partner_ref.at[number], chosen_ref, sem)
    copy.start()
    copy.wait()


def choose(partner, slice_bits):
    _, rows, cols = partner.shape
    return pl.pallas_call(
        slice_kernel,
        out_shape=pltpu.VMEM((rows, cols), F32),
        in_specs=[pl.BlockSpec(memory_space=pltpu.SMEM), pl.BlockSpec(memory_space=pl.ANY)],
        out_specs=pl.BlockSpec(memory_space=pltpu.VMEM),
        scratch_shapes=[pltpu.SemaphoreType.DMA],
    )(slice_bits, partner)


def split2(x):
    hi = x.astype(BF16)
    return hi, (x - hi.astype(F32)).astype(BF16)


def dot_nt(a, b):
    return lax.dot_general(a, b, (((1,), (1,)), ((), ())), preferred_element_type=F32)


HALVES = 2


def kernel(wides, order_ref, gate_ref, amp_ref, chosen_ref, out_ref,
           send_a, rows_in, mixed, mixed_in, mix_hi, mix_lo, held,
           own_sem, z_send, side_send, y_send, first_send, held_recv,
           a_send, a_recv, ax_send, ax_recv, m_send, m_recv, near_sem):
    me = lax.axis_index("wide")
    nar = lax.axis_index("narrow")
    lines = wides // 2
    zs_per = lines // 4
    z, y = me // 2, me % 2
    x, c = nar // 2, nar % 2
    rows, cols = amp_ref.shape
    out_bits, low_rows, wide_cols = out_ref.shape
    block = held.shape[2]
    half = block // HALVES
    flat = out_bits * low_rows

    def dev(zz, yy, xx, cc):
        return (zz * 2 + yy, xx * 2 + cc)

    core_peer = dev(z, y, x, 1 - c)

    def rc(src, dst, ssem, rsem, device):
        return pltpu.make_async_remote_copy(
            src_ref=src, dst_ref=dst, send_sem=ssem, recv_sem=rsem,
            device_id=device, device_id_type=MESH)

    barrier = pltpu.get_barrier_semaphore()

    def greet(device):
        pl.semaphore_signal(barrier, inc=1, device_id=device, device_id_type=MESH)

    def near_z(do):
        pl.when(z > 0)(lambda: do(z - 1))
        pl.when(z < lines - 1)(lambda: do(z + 1))

    greet(core_peer)
    for cc in range(2):
        greet(dev(z, 1 - y, x, cc))
        greet(dev(z, y, 1 - x, cc))
        near_z(lambda zz: greet(dev(zz, y, x, cc)))

    row_ids = lax.broadcasted_iota(jnp.int32, (rows, 128), 0)
    source = jnp.zeros((rows, 128), jnp.int32)
    for j in range(order_ref.shape[0]):
        source = source + (lax.shift_right_logical(row_ids, jnp.broadcast_to(order_ref[j], row_ids.shape)) & 1) * (1 << j)
    lane = lax.broadcasted_iota(jnp.int32, (rows, 128), 1)
    onehot = jnp.concatenate(
        [jnp.where(lane + t * 128 == source, 1.0, 0.0).astype(BF16) for t in range(rows // 128)], axis=1)
    amp = amp_ref[...]
    a1 = amp.astype(BF16)
    rest = amp - a1.astype(F32)
    a2 = rest.astype(BF16)
    a3 = (rest - a2.astype(F32)).astype(BF16)
    moved = (jnp.dot(onehot, a3, preferred_element_type=F32)
             + jnp.dot(onehot, a2, preferred_element_type=F32)
             + jnp.dot(onehot, a1, preferred_element_type=F32))
    send_a[...] = moved.reshape(send_a.shape)

    ends = jnp.where(z > 0, 1, 0) + jnp.where(z < lines - 1, 1, 0)
    pl.semaphore_wait(barrier, 5 + 2 * ends)

    quarter0 = z // zs_per
    x0, c0 = quarter0 // 2, quarter0 % 2
    j0 = (z % zs_per) * 2 + y
    cross0 = (x0 + x) % 2
    slot0 = (1 - cross0) * (2 * x) + cross0 * 4 + c

    def part(p):
        return pl.ds(p * half, half)

    def own(way, device, slot, p):
        return rc(chosen_ref.at[part(p)], held.at[slot, j0, part(p)], first_send.at[way, p], held_recv.at[slot, j0, p], device)

    def own_up(p):
        return own(0, dev((z + 1) % lines, y, x, c0), slot0, p)

    def own_down(p):
        return own(1, dev((z + lines - 1) % lines, y, x, c0), slot0, p)

    def own_side(p):
        return own(2, dev(z, (y + 1 - cross0) % 2, (x + cross0) % 2, c0), x * 2 + c, p)

    def own_core(p):
        return own(3, core_peer, x * 2 + c, p)

    own_copy = pltpu.make_async_copy(chosen_ref, held.at[x * 2 + c, j0], own_sem)
    for p in range(HALVES):
        pl.when(z < lines - 1)(lambda: own_up(p).start())
        pl.when(z > 0)(lambda: own_down(p).start())
        own_side(p).start()
    here = cross0 == 0

    @pl.when(here & (c0 != c))
    def _():
        for p in range(HALVES):
            own_core(p).start()

    @pl.when(here & (c0 == c))
    def _():
        own_copy.start()

    def a_out(zz, yy):
        to = zz * 2 + yy
        return rc(send_a.at[to], rows_in.at[x, me], a_send.at[to], a_recv.at[me], (to, nar))

    def a_in(frm):
        return rc(send_a.at[frm], rows_in.at[x, frm], a_send.at[frm], a_recv.at[frm], (frm, nar))

    def ax_out(h):
        return rc(rows_in.at[x, h], rows_in.at[x, h], ax_send.at[h], ax_recv.at[h], dev(z, y, 1 - x, c))

    def ax_in(h):
        return rc(rows_in.at[1 - x, h], rows_in.at[1 - x, h], ax_send.at[h], ax_recv.at[h], dev(z, y, 1 - x, c))

    def at(d, do):
        def line(dd, yy):
            pl.when(z - dd >= 0)(lambda: do(z - dd, yy))
            pl.when(z + dd < lines)(lambda: do(z + dd, yy))
        if isinstance(d, int) and d == 1:
            do(z, 1 - y)
        else:
            line(d - 1, 1 - y)
        line(d, y)

    rows_in[x, me] = send_a[me]
    ax_out(me).start()
    at(1, lambda zz, yy: a_out(zz, yy).start())

    def tell(r):
        def signal(device):
            pl.semaphore_signal(near_sem.at[r - 2], inc=1, device_id=device, device_id_type=MESH)
        signal(dev(z, 1 - y, x, c))
        near_z(lambda zz: signal(dev(zz, y, x, c)))

    def heard(r):
        pl.semaphore_wait(near_sem.at[r - 2], 1 + ends)
        at(r, lambda zz, yy: a_out(zz, yy).start())

    def pass_rows(d):
        def one(zz, yy):
            h = zz * 2 + yy
            a_in(h).wait_recv()
            ax_out(h).start()
        at(d, one)

    def travel(zb, cb, p, to_z):
        q = zb // zs_per
        cross = (q // 2 + x) % 2
        i = zb % zs_per
        slot = (1 - cross) * (2 * x) + cross * 4 + cb
        src = held.at[slot, i * 2 + y, part(p)]
        on = rc(src, src, z_send.at[slot, i, p], held_recv.at[slot, i * 2 + y, p], dev(to_z % lines, y, x, c))
        side = rc(src, held.at[x * 2 + cb, i * 2 + y, part(p)], side_send.at[slot, i, p],
                  held_recv.at[x * 2 + cb, i * 2 + y, p],
                  dev(z, (y + 1 - cross) % 2, (x + cross) % 2, c))
        return on, side

    def line_step(d):
        def go(zb, to_z, more):
            for p in range(HALVES):
                for cb in range(2):
                    on, side = travel(zb, cb, p, to_z)
                    on.wait_recv()
                    pl.when(more)(lambda: on.start())
                    side.start()
        pl.when((z - d >= 0) & (((z - d + lines) // zs_per) % 2 == c))(lambda: go(z - d, z + 1, z < lines - 1))
        pl.when((z + d < lines) & (((z + d) // zs_per) % 2 == c))(lambda: go(z + d, z - 1 + lines, z > 0))

    def over_y(zb, cb, p):
        i = zb % zs_per
        slot = (1 - x) * 2 + cb
        src = held.at[slot, i * 2 + y, part(p)]
        return rc(src, src, y_send.at[i, cb, p], held_recv.at[slot, i * 2 + y, p], dev(z, 1 - y, x, c))

    def x_step(d):
        def go(zb):
            for p in range(HALVES):
                for cb in range(2):
                    copy = over_y(zb, cb, p)
                    copy.wait_recv()
                    copy.start()
        pl.when((z - d >= 0) & ((z - d + lines) // zs_per == nar + 4))(lambda: go(z - d))
        if not (isinstance(d, int) and d == 0):
            pl.when((z + d < lines) & ((z + d) // zs_per == nar))(lambda: go(z + d))

    def mix(xb):
        @pl.loop(0, out_bits)
        def _(q):
            acc = gate_ref[q, 0] * rows_in[xb, 0]
            for h in range(1, wides):
                acc = acc + gate_ref[q, h] * rows_in[xb, h]
            mixed[xb, pl.ds(pl.multiple_of(q * low_rows, 8), low_rows)] = acc

    def to_core(xb):
        return rc(mixed.at[xb], mixed_in.at[xb], m_send.at[xb], m_recv.at[xb], core_peer)

    def keep(xb, cc, value):
        hi, lo = split2(value)
        mix_hi[xb * 2 + cc] = hi
        mix_lo[xb * 2 + cc] = lo

    def arrived(slot, yb, i):
        for p in range(HALVES):
            src = held.at[slot, i * 2 + yb, part(p)]
            rc(src, src, y_send.at[i, 0, p], held_recv.at[slot, i * 2 + yb, p], core_peer).wait_recv()

    def times(slot, b):
        bh, bl = split2(b)
        mh, ml = mix_hi[slot], mix_lo[slot]
        return dot_nt(jnp.concatenate([mh, ml, mh], axis=1), jnp.concatenate([bl, bh, bh], axis=1))

    def add(slot, yb, first):
        if zs_per == 1:
            at_n = pl.ds(pl.multiple_of(yb * block, 128), block)
            value = times(slot, held[slot, yb]).reshape(out_bits, low_rows, block)
        else:
            at_n = slice(None)
            value = times(slot, held[slot].reshape(wide_cols, cols)).reshape(out_ref.shape)
        if first:
            out_ref[:, :, at_n] = value
        else:
            out_ref[:, :, at_n] = out_ref[:, :, at_n] + value

    def last_own():
        @pl.when(here & (c0 == c))
        def _():
            own_copy.wait()
            arrived(x * 2 + 1 - c, y, z % zs_per)

    def others(i, slots):
        for xb in slots:
            for cb in range(2):
                arrived(xb * 2 + cb, 1 - y, i)

    tell(2)
    heard(2)
    if lines == 4:
        tell(3)
        line_step(1)
        heard(3)
        tell(4)
        x_step(0)
        pass_rows(1)
        heard(4)
        line_step(2)
        x_step(1)
        pass_rows(2)
        pass_rows(3)
        line_step(3)
        pass_rows(4)
        mix(x)
        to_core(x).start()
        x_step(2)
        x_step(3)
    else:
        @pl.loop(3, lines + 1)
        def _(r):
            tell(r)
            heard(r)

        x_step(0)

        @pl.loop(1, lines)
        def _(d):
            line_step(d)
            x_step(d)
        pass_rows(1)

        @pl.loop(2, lines + 1)
        def _(d):
            pass_rows(d)
        mix(x)
        to_core(x).start()

    ax_in(me).wait_recv()

    @pl.loop(1, wides)
    def _(s):
        ax_in((me + s) % wides).wait_recv()
    mix(1 - x)
    to_core(1 - x).start()
    keep(x, c, mixed[x])
    keep(1 - x, c, mixed[1 - x])
    for xb in (x, 1 - x):
        to_core(xb).wait_recv()
        keep(xb, 1 - c, mixed_in[xb])
    last_own()
    if zs_per == 1:
        for n, xb in enumerate((x, 1 - x)):
            for cb in range(2):
                add(xb * 2 + cb, y, n + cb == 0)
        for n, xb in enumerate((x, 1 - x)):
            for cb in range(2):
                arrived(xb * 2 + cb, 1 - y, 0)
                add(xb * 2 + cb, 1 - y, n + cb == 0)
    else:
        for n, xb in enumerate((x, 1 - x)):
            @pl.loop(0, zs_per)
            def _(i):
                others(i, (xb,))
            for cb in range(2):
                add(xb * 2 + cb, 0, n + cb == 0)

    for xb in (x, 1 - x):
        to_core(xb).wait_send()

    @pl.loop(0, wides)
    def _(h):
        ax_out(h).wait_send()

    @pl.loop(1, wides)
    def _(s):
        to = (me + s) % wides
        a_out(to // 2, to % 2).wait_send()
    for p in range(HALVES):
        pl.when(z < lines - 1)(lambda: own_up(p).wait_send())
        pl.when(z > 0)(lambda: own_down(p).wait_send())
        own_side(p).wait_send()
        pl.when(here & (c0 != c))(lambda: own_core(p).wait_send())

    def sent(d):
        def go(zb, more):
            for p in range(HALVES):
                for cb in range(2):
                    on, side = travel(zb, cb, p, z)
                    pl.when(more)(lambda: on.wait_send())
                    side.wait_send()
        pl.when((z - d >= 0) & (((z - d + lines) // zs_per) % 2 == c))(lambda: go(z - d, z < lines - 1))
        pl.when((z + d < lines) & (((z + d) // zs_per) % 2 == c))(lambda: go(z + d, z > 0))

    @pl.loop(1, lines)
    def _(d):
        sent(d)

    @pl.loop(0, zs_per)
    def _(i):
        for p in range(HALVES):
            for cb in range(2):
                over_y(nar * zs_per + i, cb, p).wait_send()


def solution(mesh):
    wides = mesh.shape["wide"]

    def per_device(amplitudes, partner, gate_block, slice_bits, bit_order):
        chosen = choose(partner, slice_bits)
        rows, cols = amplitudes.shape[1:]
        out_bits = gate_block.shape[0]
        low_rows = rows // wides
        block = chosen.shape[0]
        own = block * wides // mesh.shape["narrow"]
        flat = out_bits * low_rows
        smem = pl.BlockSpec(memory_space=pltpu.SMEM)
        vmem = pl.BlockSpec(memory_space=pltpu.VMEM)
        dma = pltpu.SemaphoreType.DMA
        lines = wides // 2
        zs_per = lines // 4
        return pl.pallas_call(
            functools.partial(kernel, wides),
            out_shape=jax.ShapeDtypeStruct((out_bits, low_rows, own), F32),
            in_specs=[smem, smem, vmem, vmem],
            out_specs=vmem,
            scratch_shapes=[
                pltpu.VMEM((wides, low_rows, cols), F32),
                pltpu.VMEM((2, wides, low_rows, cols), F32),
                pltpu.VMEM((2, flat, cols), F32),
                pltpu.VMEM((2, flat, cols), F32),
                pltpu.VMEM((4, flat, cols), BF16),
                pltpu.VMEM((4, flat, cols), BF16),
                pltpu.VMEM((6, zs_per * 2, block, cols), F32),
                dma,
                dma((6, zs_per, HALVES)), dma((6, zs_per, HALVES)), dma((zs_per, 2, HALVES)),
                dma((4, HALVES)), dma((6, zs_per * 2, HALVES)),
                dma((wides,)), dma((wides,)), dma((wides,)), dma((wides,)),
                dma((2,)), dma((2,)),
                pltpu.SemaphoreType.REGULAR((lines,)),
            ],
            compiler_params=pltpu.CompilerParams(
                collective_id=0, has_side_effects=True, vmem_limit_bytes=48 * 1024 * 1024),
        )(bit_order, gate_block, amplitudes[0], chosen)

    placed = (P("wide", None, "narrow"), P(None, "wide", "narrow"), P(), P(), P())
    return jax.shard_map(
        per_device, mesh=mesh, in_specs=placed, out_specs=P(None, "wide", "narrow"), check_vma=False
    )
```

```python
import functools

import jax
import jax.numpy as jnp
from jax import lax
from jax.experimental import pallas as pl
from jax.experimental.pallas import tpu as pltpu
from jax.sharding import PartitionSpec as P

F32 = jnp.float32
BF16 = jnp.bfloat16
MESH = pl.DeviceIdType.MESH


def slice_kernel(bits_ref, partner_ref, chosen_ref, sem):
    number = bits_ref[0]
    for j in range(1, bits_ref.shape[0]):
        number = number + bits_ref[j] * (1 << j)
    copy = pltpu.make_async_copy(partner_ref.at[number], chosen_ref, sem)
    copy.start()
    copy.wait()


def choose(partner, slice_bits):
    _, rows, cols = partner.shape
    return pl.pallas_call(
        slice_kernel,
        out_shape=pltpu.VMEM((rows, cols), F32),
        in_specs=[pl.BlockSpec(memory_space=pltpu.SMEM), pl.BlockSpec(memory_space=pl.ANY)],
        out_specs=pl.BlockSpec(memory_space=pltpu.VMEM),
        scratch_shapes=[pltpu.SemaphoreType.DMA],
    )(slice_bits, partner)


def split2(x):
    hi = x.astype(BF16)
    return hi, (x - hi.astype(F32)).astype(BF16)


def dot_nt(a, b):
    return lax.dot_general(a, b, (((1,), (1,)), ((), ())), preferred_element_type=F32)


HALVES = 4

ORDERS = {
    (0, 0, 0): ('BBBBBhBTBTBasTsTaaTaTTsaaamTn', '4216357', '231'),
    (0, 0, 1): ('IIIIhIIaBBITBIBaaBaBssTsTaTBaaBTmTTnT', '2164375', '231'),
    (0, 1, 0): ('IIhaBaIaIaBIBsBIssBIaBaBaImnB', '1462537', '231'),
    (0, 1, 1): ('TTTTTTahTaaITssaBIIsaBaIIaBmIIInBBBBB', '1264735', '231'),
    (1, 0, 0): ('ITITTThIIITTIBTTBaaBIIaaBssBBBasBaamn', '0436751', '032'),
    (1, 0, 1): ('hBBBBBBBTaBasTaaTsTTsTTaTaamn', '0643175', '302'),
    (1, 1, 0): ('TITITITIThaBTIITIBTBBBaBaIsssaaaBBamn', '3461057', '023'),
    (1, 1, 1): ('haIaaIBIssIBIBasIaIBIBBBaBamn', '3046175', '302'),
}


def tables():
    orders, row_words, stage_words = [], [], []
    for z in range(4):
        for x in range(2):
            for c in range(2):
                flip = z >= 2
                order, rows, stages = ORDERS[(3 - z, 1 - x, 1 - c) if flip else (z, x, c)]
                rows = [(3 - int(r) // 2) * 2 + int(r) % 2 if flip else int(r) for r in rows]
                stages = [3 - int(r) if flip else int(r) for r in stages]
                orders.append([" ITBashmn".index(e) for e in order])
                row_words.append(sum(r * 8 ** k for k, r in enumerate(rows)))
                stage_words.append(sum(r * 4 ** k for k, r in enumerate(stages)))
    length = -(-max(len(o) for o in orders) // 7)
    words = [[sum(e * 16 ** k for k, e in enumerate(o[w * 7:w * 7 + 7])) for o in orders] for w in range(length)]
    return words, row_words, stage_words


def kernel(wides, order_ref, gate_ref, amp_ref, chosen_ref, out_ref,
           send_a, staged, rows_in, mixed, mixed_in, mix_hi, mix_lo, held,
           own_sem, z_send, side_send, y_send, first_send, held_recv,
           a_send, a_recv, st_send, st_recv, sf_send, ax_send, ax_recv, m_send, m_recv, near_sem):
    me = lax.axis_index("wide")
    nar = lax.axis_index("narrow")
    lines = wides // 2
    zs_per = lines // 4
    z, y = me // 2, me % 2
    x, c = nar // 2, nar % 2
    rows, cols = amp_ref.shape
    out_bits, low_rows, wide_cols = out_ref.shape
    block = held.shape[2]
    half = block // HALVES
    flat = out_bits * low_rows

    def dev(zz, yy, xx, cc):
        return (zz * 2 + yy, xx * 2 + cc)

    core_peer = dev(z, y, x, 1 - c)

    def rc(src, dst, ssem, rsem, device):
        return pltpu.make_async_remote_copy(
            src_ref=src, dst_ref=dst, send_sem=ssem, recv_sem=rsem,
            device_id=device, device_id_type=MESH)

    barrier = pltpu.get_barrier_semaphore()

    def greet(device):
        pl.semaphore_signal(barrier, inc=1, device_id=device, device_id_type=MESH)

    def near_z(do):
        pl.when(z > 0)(lambda: do(z - 1))
        pl.when(z < lines - 1)(lambda: do(z + 1))

    greet(core_peer)
    for cc in range(2):
        greet(dev(z, 1 - y, x, cc))
        greet(dev(z, y, 1 - x, cc))
        near_z(lambda zz: greet(dev(zz, y, x, cc)))

    row_ids = lax.broadcasted_iota(jnp.int32, (rows, 128), 0)
    source = jnp.zeros((rows, 128), jnp.int32)
    for j in range(order_ref.shape[0]):
        source = source + (lax.shift_right_logical(row_ids, jnp.broadcast_to(order_ref[j], row_ids.shape)) & 1) * (1 << j)
    lane = lax.broadcasted_iota(jnp.int32, (rows, 128), 1)
    onehot = jnp.concatenate(
        [jnp.where(lane + t * 128 == source, 1.0, 0.0).astype(BF16) for t in range(rows // 128)], axis=1)
    amp = amp_ref[...]
    a1 = amp.astype(BF16)
    rest = amp - a1.astype(F32)
    a2 = rest.astype(BF16)
    a3 = (rest - a2.astype(F32)).astype(BF16)
    moved = (jnp.dot(onehot, a3, preferred_element_type=F32)
             + jnp.dot(onehot, a2, preferred_element_type=F32)
             + jnp.dot(onehot, a1, preferred_element_type=F32))
    send_a[...] = moved.reshape(send_a.shape)

    ends = jnp.where(z > 0, 1, 0) + jnp.where(z < lines - 1, 1, 0)
    pl.semaphore_wait(barrier, 5 + 2 * ends)

    quarter0 = z // zs_per
    x0, c0 = quarter0 // 2, quarter0 % 2
    j0 = (z % zs_per) * 2 + y
    cross0 = (x0 + x) % 2
    slot0 = (1 - cross0) * (2 * x) + cross0 * 4 + c

    def part(p):
        return pl.ds(p * half, half)

    def own(way, device, slot, p):
        return rc(chosen_ref.at[part(p)], held.at[slot, j0, part(p)], first_send.at[way, p], held_recv.at[slot, j0, p], device)

    def own_up(p):
        return own(0, dev((z + 1) % lines, y, x, c0), slot0, p)

    def own_down(p):
        return own(1, dev((z + lines - 1) % lines, y, x, c0), slot0, p)

    def own_side(p):
        return own(2, dev(z, (y + 1 - cross0) % 2, (x + cross0) % 2, c0), x * 2 + c, p)

    def own_core(p):
        return own(3, core_peer, x * 2 + c, p)

    own_copy = pltpu.make_async_copy(chosen_ref, held.at[x * 2 + c, j0], own_sem)
    here = cross0 == 0
    rows_in[x, me] = send_a[me]

    def a_out(zz, yy):
        to = zz * 2 + yy
        return rc(send_a.at[to], rows_in.at[x, me], a_send.at[to], a_recv.at[me], (to, nar))

    def a_in(frm):
        return rc(send_a.at[frm], rows_in.at[x, frm], a_send.at[frm], a_recv.at[frm], (frm, nar))

    def stage(zz):
        return rc(send_a.at[zz * 2 + 1 - y], staged.at[zz], st_send.at[zz], st_recv.at[zz], dev(z, 1 - y, x, c))

    def stage_on(zz):
        frm = z * 2 + 1 - y
        return rc(staged.at[zz], rows_in.at[x, frm], sf_send.at[zz], a_recv.at[frm], dev(zz, y, x, c))

    def ax_out(h):
        return rc(rows_in.at[x, h], rows_in.at[x, h], ax_send.at[h], ax_recv.at[h], dev(z, y, 1 - x, c))

    def ax_in(h):
        return rc(rows_in.at[1 - x, h], rows_in.at[1 - x, h], ax_send.at[h], ax_recv.at[h], dev(z, y, 1 - x, c))

    def line(d, do):
        pl.when(z - d >= 0)(lambda: do(z - d))
        pl.when(z + d < lines)(lambda: do(z + d))

    def each_line(do):
        if lines == 4:
            for d in range(lines - 1, 0, -1):
                line(d, do)
        else:
            @pl.loop(1, lines)
            def _(d):
                line(d, do)

    for p in range(HALVES):
        pl.when(z < lines - 1)(lambda: own_up(p).start())
        pl.when(z > 0)(lambda: own_down(p).start())
        own_side(p).start()
    each_line(lambda zz: stage(zz).start())
    a_out(z, 1 - y).start()
    ax_out(me).start()

    @pl.when(here & (c0 != c))
    def _():
        for p in range(HALVES):
            own_core(p).start()

    @pl.when(here & (c0 == c))
    def _():
        own_copy.start()

    def tell(r):
        near_z(lambda zz: pl.semaphore_signal(
            near_sem.at[r - 2], inc=1, device_id=dev(zz, y, x, c), device_id_type=MESH))

    def heard(r):
        pl.semaphore_wait(near_sem.at[r - 2], ends)

    def forward_stage():
        def one(zz):
            stage(zz).wait_recv()
            stage_on(zz).start()
        each_line(one)

    def pass_one(zz, yy):
        h = zz * 2 + yy
        a_in(h).wait_recv()
        ax_out(h).start()

    def pass_rows(d):
        line(d, lambda zz: pass_one(zz, y))
        line(d, lambda zz: pass_one(zz, 1 - y))

    def travel(zb, cb, p, to_z):
        q = zb // zs_per
        cross = (q // 2 + x) % 2
        i = zb % zs_per
        slot = (1 - cross) * (2 * x) + cross * 4 + cb
        src = held.at[slot, i * 2 + y, part(p)]
        on = rc(src, src, z_send.at[slot, i, p], held_recv.at[slot, i * 2 + y, p], dev(to_z % lines, y, x, c))
        side = rc(src, held.at[x * 2 + cb, i * 2 + y, part(p)], side_send.at[slot, i, p],
                  held_recv.at[x * 2 + cb, i * 2 + y, p],
                  dev(z, (y + 1 - cross) % 2, (x + cross) % 2, c))
        return on, side

    def take(zb, cb, p, to_z, more):
        on, side = travel(zb, cb, p, to_z)
        on.wait_recv()
        pl.when(more)(lambda: on.start())
        side.start()

    def line_step(d):
        def go(zb, to_z, more):
            for p in range(HALVES):
                for cb in range(2):
                    take(zb, cb, p, to_z, more)
        pl.when((z - d >= 0) & (((z - d + lines) // zs_per) % 2 == c))(lambda: go(z - d, z + 1, z < lines - 1))
        pl.when((z + d < lines) & (((z + d) // zs_per) % 2 == c))(lambda: go(z + d, z - 1 + lines, z > 0))

    def over_y(zb, cb, p):
        i = zb % zs_per
        slot = (1 - x) * 2 + cb
        src = held.at[slot, i * 2 + y, part(p)]
        return rc(src, src, y_send.at[i, cb, p], held_recv.at[slot, i * 2 + y, p], dev(z, 1 - y, x, c))

    def take_x(zb, cb, p):
        copy = over_y(zb, cb, p)
        copy.wait_recv()
        copy.start()

    def x_step(d):
        def go(zb):
            for p in range(HALVES):
                for cb in range(2):
                    take_x(zb, cb, p)
        pl.when((z - d >= 0) & ((z - d + lines) // zs_per == nar + 4))(lambda: go(z - d))
        if not (isinstance(d, int) and d == 0):
            pl.when((z + d < lines) & ((z + d) // zs_per == nar))(lambda: go(z + d))

    def mix(xb):
        @pl.loop(0, out_bits)
        def _(q):
            acc = gate_ref[q, 0] * rows_in[xb, 0]
            for h in range(1, wides):
                acc = acc + gate_ref[q, h] * rows_in[xb, h]
            mixed[xb, pl.ds(pl.multiple_of(q * low_rows, 8), low_rows)] = acc

    def to_core(xb):
        return rc(mixed.at[xb], mixed_in.at[xb], m_send.at[xb], m_recv.at[xb], core_peer)

    def keep(xb, cc, value):
        hi, lo = split2(value)
        mix_hi[xb * 2 + cc] = hi
        mix_lo[xb * 2 + cc] = lo

    def arrived(slot, yb, i):
        for p in range(HALVES):
            src = held.at[slot, i * 2 + yb, part(p)]
            rc(src, src, y_send.at[i, 0, p], held_recv.at[slot, i * 2 + yb, p], core_peer).wait_recv()

    def times(slot, b):
        bh, bl = split2(b)
        mh, ml = mix_hi[slot], mix_lo[slot]
        return dot_nt(jnp.concatenate([mh, ml, mh], axis=1), jnp.concatenate([bl, bh, bh], axis=1))

    def add(slot, yb, first):
        if zs_per == 1:
            at_n = pl.ds(pl.multiple_of(yb * block, 128), block)
            value = times(slot, held[slot, yb]).reshape(out_bits, low_rows, block)
        else:
            at_n = slice(None)
            value = times(slot, held[slot].reshape(wide_cols, cols)).reshape(out_ref.shape)
        if first:
            out_ref[:, :, at_n] = value
        else:
            out_ref[:, :, at_n] = out_ref[:, :, at_n] + value

    def last_own():
        @pl.when(here & (c0 == c))
        def _():
            own_copy.wait()
            arrived(x * 2 + 1 - c, y, z % zs_per)

    def others(i, slots):
        for xb in slots:
            for cb in range(2):
                arrived(xb * 2 + cb, 1 - y, i)

    def mix_near():
        mix(x)
        to_core(x).start()

    def mix_far():
        ax_in(me).wait_recv()

        @pl.loop(1, wides)
        def _(s):
            ax_in((me + s) % wides).wait_recv()
        mix(1 - x)
        to_core(1 - x).start()

    tell(2)
    heard(2)
    if lines == 4:
        tell(3)
        place = z * 4 + x * 2 + c
        words, rows_word, stage_word = tables()

        def pick(values):
            if len(set(values)) == 1:
                return jnp.int32(values[0])
            word = jnp.int32(values[0])
            for k in range(1, len(values)):
                word = jnp.where(place == k, values[k], word)
            return word

        steps = [pick(v) for v in words]
        other = (1 - x) * 2 + c

        def passing(zb, n):
            below = zb < z
            take(zb, n % 2, n // 2, jnp.where(below, z + 1, z + 3), jnp.where(below, z < lines - 1, z > 0))

        def event(_, carry):
            word, ni, nt, nb, a_word, s_word = carry
            kind = word % 16

            @pl.when(kind == 1)
            def _():
                passing(nar, ni)

            @pl.when(kind == 2)
            def _():
                passing(other, nt)

            @pl.when(kind == 3)
            def _():
                take_x(nar, nb % 2, nb // 2)

            @pl.when(kind == 4)
            def _():
                pass_one(a_word % 8 // 2, (y + a_word) % 2)

            @pl.when(kind == 5)
            def _():
                zz = s_word % 4
                stage(zz).wait_recv()
                stage_on(zz).start()

            @pl.when(kind == 6)
            def _():
                heard(3)
                each_line(lambda zz: a_out(zz, y).start())

            @pl.when(kind == 7)
            def _():
                mix_near()

            @pl.when(kind == 8)
            def _():
                mix_far()
            one = lambda k: jnp.where(kind == k, 1, 0)
            return (word // 16, ni + one(1), nt + one(2), nb + one(3),
                    jnp.where(kind == 4, a_word // 8, a_word), jnp.where(kind == 5, s_word // 4, s_word))

        def stretch(w, carry):
            word = steps[0]
            for k in range(1, len(steps)):
                word = jnp.where(w == k, steps[k], word)
            return lax.fori_loop(0, 7, event, (word, *carry))[1:]

        zero = jnp.int32(0)
        lax.fori_loop(0, len(steps), stretch, (zero, zero, zero, pick(rows_word), pick(stage_word)))
    else:
        @pl.loop(3, lines)
        def _(r):
            tell(r)
            heard(r)

        x_step(0)
        each_line(lambda zz: a_out(zz, y).start())
        forward_stage()

        @pl.loop(1, lines)
        def _(d):
            line_step(d)
            x_step(d)
        pass_one(z, 1 - y)

        @pl.loop(1, lines)
        def _(d):
            pass_rows(d)
        mix_near()
        mix_far()
    keep(x, c, mixed[x])
    keep(1 - x, c, mixed[1 - x])
    for xb in (x, 1 - x):
        to_core(xb).wait_recv()
        keep(xb, 1 - c, mixed_in[xb])
    last_own()
    if zs_per == 1:
        for n, xb in enumerate((x, 1 - x)):
            for cb in range(2):
                add(xb * 2 + cb, y, n + cb == 0)
        for n, xb in enumerate((x, 1 - x)):
            for cb in range(2):
                arrived(xb * 2 + cb, 1 - y, 0)
                add(xb * 2 + cb, 1 - y, n + cb == 0)
    else:
        for n, xb in enumerate((x, 1 - x)):
            @pl.loop(0, zs_per)
            def _(i):
                others(i, (xb,))
            for cb in range(2):
                add(xb * 2 + cb, 0, n + cb == 0)

    for xb in (x, 1 - x):
        to_core(xb).wait_send()

    @pl.loop(0, wides)
    def _(h):
        ax_out(h).wait_send()

    a_out(z, 1 - y).wait_send()

    @pl.loop(1, lines)
    def _(s):
        zz = (z + s) % lines
        a_out(zz, y).wait_send()
        stage(zz).wait_send()
        stage_on(zz).wait_send()
    for p in range(HALVES):
        pl.when(z < lines - 1)(lambda: own_up(p).wait_send())
        pl.when(z > 0)(lambda: own_down(p).wait_send())
        own_side(p).wait_send()
        pl.when(here & (c0 != c))(lambda: own_core(p).wait_send())

    def sent(d):
        def go(zb, more):
            for p in range(HALVES):
                for cb in range(2):
                    on, side = travel(zb, cb, p, z)
                    pl.when(more)(lambda: on.wait_send())
                    side.wait_send()
        pl.when((z - d >= 0) & (((z - d + lines) // zs_per) % 2 == c))(lambda: go(z - d, z < lines - 1))
        pl.when((z + d < lines) & (((z + d) // zs_per) % 2 == c))(lambda: go(z + d, z > 0))

    @pl.loop(1, lines)
    def _(d):
        sent(d)

    @pl.loop(0, zs_per)
    def _(i):
        for p in range(HALVES):
            for cb in range(2):
                over_y(nar * zs_per + i, cb, p).wait_send()


def solution(mesh):
    wides = mesh.shape["wide"]

    def per_device(amplitudes, partner, gate_block, slice_bits, bit_order):
        chosen = choose(partner, slice_bits)
        rows, cols = amplitudes.shape[1:]
        out_bits = gate_block.shape[0]
        low_rows = rows // wides
        block = chosen.shape[0]
        own = block * wides // mesh.shape["narrow"]
        flat = out_bits * low_rows
        smem = pl.BlockSpec(memory_space=pltpu.SMEM)
        vmem = pl.BlockSpec(memory_space=pltpu.VMEM)
        dma = pltpu.SemaphoreType.DMA
        lines = wides // 2
        zs_per = lines // 4
        return pl.pallas_call(
            functools.partial(kernel, wides),
            out_shape=jax.ShapeDtypeStruct((out_bits, low_rows, own), F32),
            in_specs=[smem, smem, vmem, vmem],
            out_specs=vmem,
            scratch_shapes=[
                pltpu.VMEM((wides, low_rows, cols), F32),
                pltpu.VMEM((lines, low_rows, cols), F32),
                pltpu.VMEM((2, wides, low_rows, cols), F32),
                pltpu.VMEM((2, flat, cols), F32),
                pltpu.VMEM((2, flat, cols), F32),
                pltpu.VMEM((4, flat, cols), BF16),
                pltpu.VMEM((4, flat, cols), BF16),
                pltpu.VMEM((6, zs_per * 2, block, cols), F32),
                dma,
                dma((6, zs_per, HALVES)), dma((6, zs_per, HALVES)), dma((zs_per, 2, HALVES)),
                dma((4, HALVES)), dma((6, zs_per * 2, HALVES)),
                dma((wides,)), dma((wides,)), dma((lines,)), dma((lines,)), dma((lines,)), dma((wides,)), dma((wides,)),
                dma((2,)), dma((2,)),
                pltpu.SemaphoreType.REGULAR((lines,)),
            ],
            compiler_params=pltpu.CompilerParams(
                collective_id=0, has_side_effects=True, vmem_limit_bytes=48 * 1024 * 1024),
        )(bit_order, gate_block, amplitudes[0], chosen)

    placed = (P("wide", None, "narrow"), P(None, "wide", "narrow"), P(), P(), P())
    return jax.shard_map(
        per_device, mesh=mesh, in_specs=placed, out_specs=P(None, "wide", "narrow"), check_vma=False
    )
```

```python
import functools

import jax
import jax.numpy as jnp
from jax import lax
from jax.experimental import pallas as pl
from jax.experimental.pallas import tpu as pltpu
from jax.sharding import PartitionSpec as P

F32 = jnp.float32
BF16 = jnp.bfloat16
MESH = pl.DeviceIdType.MESH


def slice_kernel(bits_ref, partner_ref, chosen_ref, sem):
    number = bits_ref[0]
    for j in range(1, bits_ref.shape[0]):
        number = number + bits_ref[j] * (1 << j)
    copy = pltpu.make_async_copy(partner_ref.at[number], chosen_ref, sem)
    copy.start()
    copy.wait()


def choose(partner, slice_bits):
    _, rows, cols = partner.shape
    return pl.pallas_call(
        slice_kernel,
        out_shape=pltpu.VMEM((rows, cols), F32),
        in_specs=[pl.BlockSpec(memory_space=pltpu.SMEM), pl.BlockSpec(memory_space=pl.ANY)],
        out_specs=pl.BlockSpec(memory_space=pltpu.VMEM),
        scratch_shapes=[pltpu.SemaphoreType.DMA],
    )(slice_bits, partner)


def split2(x):
    hi = x.astype(BF16)
    return hi, (x - hi.astype(F32)).astype(BF16)


def dot_nt(a, b):
    return lax.dot_general(a, b, (((1,), (1,)), ((), ())), preferred_element_type=F32)


HALVES = 4

ORDERS = {
    (0, 0, 0): ('BBBBBBBBTTTTThsssaTTTaaaaaampqrn', '1573426', '321'),
    (0, 0, 1): ('IIIIIIIIBBTBhsssBTBaBTBBTaTaTaaaTTampqrn', '1574632', '321'),
    (0, 1, 0): ('aIIIIBBIhsssBBIBIIBaBaBaaaampqrn', '1573426', '321'),
    (0, 1, 1): ('TTTTTTTTaIhsssIBIIBaBIBaIBaaaBIIampqBBrn', '1574632', '321'),
    (1, 0, 0): ('ITITITITITITITITBBBsssBaBBhBBaaaaaampqrn', '3157064', '302'),
    (1, 0, 1): ('BBBBBBBBTTTTTTsssTTahaaaaaampqrn', '3157064', '302'),
    (1, 1, 0): ('TITITITIBTITIBBTITIBaBBBBssshaaaaaampqrn', '3157064', '302'),
    (1, 1, 1): ('IaIIIIBIBsssIBIBhBBBBaaaaaampqrn', '3157064', '302'),
}


def tables():
    orders, row_words, stage_words = [], [], []
    for z in range(4):
        for x in range(2):
            for c in range(2):
                flip = z >= 2
                order, rows, stages = ORDERS[(3 - z, 1 - x, 1 - c) if flip else (z, x, c)]
                rows = [(3 - int(r) // 2) * 2 + int(r) % 2 if flip else int(r) for r in rows]
                stages = [3 - int(r) if flip else int(r) for r in stages]
                orders.append([" ITBashmnpqr".index(e) for e in order])
                row_words.append(sum(r * 8 ** k for k, r in enumerate(rows)))
                stage_words.append(sum(r * 4 ** k for k, r in enumerate(stages)))
    length = -(-max(len(o) for o in orders) // 7)
    words = [[sum(e * 16 ** k for k, e in enumerate(o[w * 7:w * 7 + 7])) for o in orders] for w in range(length)]
    return words, row_words, stage_words


def kernel(wides, order_ref, gate_ref, amp_ref, chosen_ref, out_ref,
           send_a, staged, rows_in, mixed, mixed_in, mix_hi, mix_lo, held,
           own_sem, z_send, side_send, y_send, first_send, held_recv,
           a_send, a_recv, st_send, st_recv, sf_send, ax_send, ax_recv, m_send, m_recv, near_sem):
    me = lax.axis_index("wide")
    nar = lax.axis_index("narrow")
    lines = wides // 2
    zs_per = lines // 4
    z, y = me // 2, me % 2
    x, c = nar // 2, nar % 2
    rows, cols = amp_ref.shape
    out_bits, low_rows, wide_cols = out_ref.shape
    block = held.shape[2]
    half = block // HALVES
    flat = out_bits * low_rows

    def dev(zz, yy, xx, cc):
        return (zz * 2 + yy, xx * 2 + cc)

    core_peer = dev(z, y, x, 1 - c)

    def rc(src, dst, ssem, rsem, device):
        return pltpu.make_async_remote_copy(
            src_ref=src, dst_ref=dst, send_sem=ssem, recv_sem=rsem,
            device_id=device, device_id_type=MESH)

    barrier = pltpu.get_barrier_semaphore()

    def greet(device):
        pl.semaphore_signal(barrier, inc=1, device_id=device, device_id_type=MESH)

    def near_z(do):
        pl.when(z > 0)(lambda: do(z - 1))
        pl.when(z < lines - 1)(lambda: do(z + 1))

    greet(core_peer)
    for cc in range(2):
        greet(dev(z, 1 - y, x, cc))
        greet(dev(z, y, 1 - x, cc))
        near_z(lambda zz: greet(dev(zz, y, x, cc)))

    row_ids = lax.broadcasted_iota(jnp.int32, (rows, 128), 0)
    source = jnp.zeros((rows, 128), jnp.int32)
    for j in range(order_ref.shape[0]):
        source = source + (lax.shift_right_logical(row_ids, jnp.broadcast_to(order_ref[j], row_ids.shape)) & 1) * (1 << j)
    lane = lax.broadcasted_iota(jnp.int32, (rows, 128), 1)
    onehot = jnp.concatenate(
        [jnp.where(lane + t * 128 == source, 1.0, 0.0).astype(BF16) for t in range(rows // 128)], axis=1)
    amp = amp_ref[...]
    a1 = amp.astype(BF16)
    rest = amp - a1.astype(F32)
    a2 = rest.astype(BF16)
    a3 = (rest - a2.astype(F32)).astype(BF16)
    moved = (jnp.dot(onehot, a3, preferred_element_type=F32)
             + jnp.dot(onehot, a2, preferred_element_type=F32)
             + jnp.dot(onehot, a1, preferred_element_type=F32))
    send_a[...] = moved.reshape(send_a.shape)

    ends = jnp.where(z > 0, 1, 0) + jnp.where(z < lines - 1, 1, 0)
    pl.semaphore_wait(barrier, 5 + 2 * ends)

    quarter0 = z // zs_per
    x0, c0 = quarter0 // 2, quarter0 % 2
    j0 = (z % zs_per) * 2 + y
    cross0 = (x0 + x) % 2
    slot0 = (1 - cross0) * (2 * x) + cross0 * 4 + c

    def part(p):
        return pl.ds(p * half, half)

    def own(way, device, slot, p):
        return rc(chosen_ref.at[part(p)], held.at[slot, j0, part(p)], first_send.at[way, p], held_recv.at[slot, j0, p], device)

    def own_up(p):
        return own(0, dev((z + 1) % lines, y, x, c0), slot0, p)

    def own_down(p):
        return own(1, dev((z + lines - 1) % lines, y, x, c0), slot0, p)

    def own_side(p):
        return own(2, dev(z, (y + 1 - cross0) % 2, (x + cross0) % 2, c0), x * 2 + c, p)

    def own_core(p):
        return own(3, core_peer, x * 2 + c, p)

    own_copy = pltpu.make_async_copy(chosen_ref, held.at[x * 2 + c, j0], own_sem)
    here = cross0 == 0
    rows_in[x, me] = send_a[me]

    def a_out(zz, yy):
        to = zz * 2 + yy
        return rc(send_a.at[to], rows_in.at[x, me], a_send.at[to], a_recv.at[me], (to, nar))

    def a_in(frm):
        return rc(send_a.at[frm], rows_in.at[x, frm], a_send.at[frm], a_recv.at[frm], (frm, nar))

    def stage(zz):
        return rc(send_a.at[zz * 2 + 1 - y], staged.at[zz], st_send.at[zz], st_recv.at[zz], dev(z, 1 - y, x, c))

    def stage_on(zz):
        frm = z * 2 + 1 - y
        return rc(staged.at[zz], rows_in.at[x, frm], sf_send.at[zz], a_recv.at[frm], dev(zz, y, x, c))

    def ax_out(h):
        return rc(rows_in.at[x, h], rows_in.at[x, h], ax_send.at[h], ax_recv.at[h], dev(z, y, 1 - x, c))

    def ax_in(h):
        return rc(rows_in.at[1 - x, h], rows_in.at[1 - x, h], ax_send.at[h], ax_recv.at[h], dev(z, y, 1 - x, c))

    def line(d, do):
        pl.when(z - d >= 0)(lambda: do(z - d))
        pl.when(z + d < lines)(lambda: do(z + d))

    def each_line(do):
        if lines == 4:
            for d in range(lines - 1, 0, -1):
                line(d, do)
        else:
            @pl.loop(1, lines)
            def _(d):
                line(d, do)

    for p in range(HALVES):
        pl.when(z < lines - 1)(lambda: own_up(p).start())
        pl.when(z > 0)(lambda: own_down(p).start())
        own_side(p).start()
    each_line(lambda zz: stage(zz).start())
    a_out(z, 1 - y).start()
    ax_out(me).start()

    @pl.when(here & (c0 != c))
    def _():
        for p in range(HALVES):
            own_core(p).start()

    @pl.when(here & (c0 == c))
    def _():
        own_copy.start()

    def tell(r):
        near_z(lambda zz: pl.semaphore_signal(
            near_sem.at[r - 2], inc=1, device_id=dev(zz, y, x, c), device_id_type=MESH))

    def heard(r):
        pl.semaphore_wait(near_sem.at[r - 2], ends)

    def forward_stage():
        def one(zz):
            stage(zz).wait_recv()
            stage_on(zz).start()
        each_line(one)

    def pass_one(zz, yy):
        h = zz * 2 + yy
        a_in(h).wait_recv()
        ax_out(h).start()

    def pass_rows(d):
        line(d, lambda zz: pass_one(zz, y))
        line(d, lambda zz: pass_one(zz, 1 - y))

    def travel(zb, cb, p, to_z):
        q = zb // zs_per
        cross = (q // 2 + x) % 2
        i = zb % zs_per
        slot = (1 - cross) * (2 * x) + cross * 4 + cb
        src = held.at[slot, i * 2 + y, part(p)]
        on = rc(src, src, z_send.at[slot, i, p], held_recv.at[slot, i * 2 + y, p], dev(to_z % lines, y, x, c))
        side = rc(src, held.at[x * 2 + cb, i * 2 + y, part(p)], side_send.at[slot, i, p],
                  held_recv.at[x * 2 + cb, i * 2 + y, p],
                  dev(z, (y + 1 - cross) % 2, (x + cross) % 2, c))
        return on, side

    def take(zb, cb, p, to_z, more):
        on, side = travel(zb, cb, p, to_z)
        on.wait_recv()
        pl.when(more)(lambda: on.start())
        side.start()

    def line_step(d):
        def go(zb, to_z, more):
            for p in range(HALVES):
                for cb in range(2):
                    take(zb, cb, p, to_z, more)
        pl.when((z - d >= 0) & (((z - d + lines) // zs_per) % 2 == c))(lambda: go(z - d, z + 1, z < lines - 1))
        pl.when((z + d < lines) & (((z + d) // zs_per) % 2 == c))(lambda: go(z + d, z - 1 + lines, z > 0))

    def over_y(zb, cb, p):
        i = zb % zs_per
        slot = (1 - x) * 2 + cb
        src = held.at[slot, i * 2 + y, part(p)]
        return rc(src, src, y_send.at[i, cb, p], held_recv.at[slot, i * 2 + y, p], dev(z, 1 - y, x, c))

    def take_x(zb, cb, p):
        copy = over_y(zb, cb, p)
        copy.wait_recv()
        copy.start()

    def x_step(d):
        def go(zb):
            for p in range(HALVES):
                for cb in range(2):
                    take_x(zb, cb, p)
        pl.when((z - d >= 0) & ((z - d + lines) // zs_per == nar + 4))(lambda: go(z - d))
        if not (isinstance(d, int) and d == 0):
            pl.when((z + d < lines) & ((z + d) // zs_per == nar))(lambda: go(z + d))

    def mix(xb):
        @pl.loop(0, out_bits)
        def _(q):
            acc = gate_ref[q, 0] * rows_in[xb, 0]
            for h in range(1, wides):
                acc = acc + gate_ref[q, h] * rows_in[xb, h]
            mixed[xb, pl.ds(pl.multiple_of(q * low_rows, 8), low_rows)] = acc

    def to_core(xb):
        return rc(mixed.at[xb], mixed_in.at[xb], m_send.at[xb], m_recv.at[xb], core_peer)

    def keep(xb, cc, value):
        hi, lo = split2(value)
        mix_hi[xb * 2 + cc] = hi
        mix_lo[xb * 2 + cc] = lo

    def arrived(slot, yb, i):
        for p in range(HALVES):
            src = held.at[slot, i * 2 + yb, part(p)]
            rc(src, src, y_send.at[i, 0, p], held_recv.at[slot, i * 2 + yb, p], core_peer).wait_recv()

    def both(slots, b):
        left, right = [], []
        for slot, value in zip(slots, b):
            bh, bl = split2(value)
            mh, ml = mix_hi[slot], mix_lo[slot]
            left += [mh, ml, mh]
            right += [bl, bh, bh]
        return dot_nt(jnp.concatenate(left, axis=1), jnp.concatenate(right, axis=1))

    def put(at_n, value, first):
        value = value.reshape(out_bits, low_rows, value.shape[1])
        if first:
            out_ref[:, :, at_n] = value
        else:
            out_ref[:, :, at_n] = out_ref[:, :, at_n] + value

    def add(slots, yb, first=False):
        if zs_per == 1:
            at_n = pl.ds(pl.multiple_of(yb * block, 128), block)
            put(at_n, both(slots, [held[slot, yb] for slot in slots]), first)
        else:
            put(slice(None), both(slots, [held[slot].reshape(wide_cols, cols) for slot in slots]), first)

    def add_two(xb, yb, first=False):
        if isinstance(first, bool) and first:
            last_own(yb)
        slots = [xb * 2, xb * 2 + 1]
        if yb is not y:
            for slot in slots:
                arrived(slot, yb, 0)
        add(slots, yb, first)

    def last_own(yb):
        if yb is y:
            @pl.when(here & (c0 == c))
            def _():
                own_copy.wait()
                arrived(x * 2 + 1 - c, y, z % zs_per)

    def others(i, slots):
        for xb in slots:
            for cb in range(2):
                arrived(xb * 2 + cb, 1 - y, i)

    def mix_near():
        mix(x)
        to_core(x).start()
        keep(x, c, mixed[x])

    def swap_near():
        to_core(x).wait_recv()
        keep(x, 1 - c, mixed_in[x])

    def mix_far():
        ax_in(me).wait_recv()

        @pl.loop(1, wides)
        def _(s):
            ax_in((me + s) % wides).wait_recv()
        mix(1 - x)
        to_core(1 - x).start()
        keep(1 - x, c, mixed[1 - x])

    tell(2)
    heard(2)
    if lines == 4:
        tell(3)
        place = z * 4 + x * 2 + c
        words, rows_word, stage_word = tables()

        def pick(values):
            if len(set(values)) == 1:
                return jnp.int32(values[0])
            word = jnp.int32(values[0])
            for k in range(1, len(values)):
                word = jnp.where(place == k, values[k], word)
            return word

        steps = [pick(v) for v in words]
        other = (1 - x) * 2 + c

        def passing(zb, n):
            below = zb < z
            take(zb, n % 2, n // 2, jnp.where(below, z + 1, z + 3), jnp.where(below, z < lines - 1, z > 0))

        def event(_, carry):
            word, ni, nt, nb, a_word, s_word = carry
            kind = word % 16

            @pl.when(kind < 4)
            def _():
                @pl.when(kind == 1)
                def _():
                    passing(nar, ni)

                @pl.when(kind == 2)
                def _():
                    passing(other, nt)

                @pl.when(kind == 3)
                def _():
                    take_x(nar, nb % 2, nb // 2)

            @pl.when((kind >= 4) & (kind < 7))
            def _():
                @pl.when(kind == 4)
                def _():
                    pass_one(a_word % 8 // 2, (y + a_word) % 2)

                @pl.when(kind == 5)
                def _():
                    zz = s_word % 4
                    stage(zz).wait_recv()
                    stage_on(zz).start()

                @pl.when(kind == 6)
                def _():
                    heard(3)
                    each_line(lambda zz: a_out(zz, y).start())

            @pl.when(kind >= 7)
            def _():
                pl.when(kind == 7)(mix_near)
                pl.when(kind == 8)(mix_far)
                pl.when(kind == 9)(swap_near)
                pl.when(kind == 10)(lambda: add_two(x, y, True))
                pl.when(kind == 11)(lambda: add_two(x, 1 - y, True))
            one = lambda k: jnp.where(kind == k, 1, 0)
            return (word // 16, ni + one(1), nt + one(2), nb + one(3),
                    jnp.where(kind == 4, a_word // 8, a_word), jnp.where(kind == 5, s_word // 4, s_word))

        def stretch(w, carry):
            word = steps[0]
            for k in range(1, len(steps)):
                word = jnp.where(w == k, steps[k], word)
            return lax.fori_loop(0, 7, event, (word, *carry))[1:]

        zero = jnp.int32(0)
        lax.fori_loop(0, len(steps), stretch, (zero, zero, zero, pick(rows_word), pick(stage_word)))
    else:
        @pl.loop(3, lines)
        def _(r):
            tell(r)
            heard(r)

        x_step(0)
        each_line(lambda zz: a_out(zz, y).start())
        forward_stage()

        @pl.loop(1, lines)
        def _(d):
            line_step(d)
            x_step(d)
        pass_one(z, 1 - y)

        @pl.loop(1, lines)
        def _(d):
            pass_rows(d)
        mix_near()
        mix_far()
        swap_near()
    def settle():
        to_core(x).wait_send()

        @pl.loop(0, wides)
        def _(h):
            ax_out(h).wait_send()

        a_out(z, 1 - y).wait_send()

        @pl.loop(1, lines)
        def _(s):
            zz = (z + s) % lines
            a_out(zz, y).wait_send()
            stage(zz).wait_send()
            stage_on(zz).wait_send()
        for p in range(HALVES):
            pl.when(z < lines - 1)(lambda: own_up(p).wait_send())
            pl.when(z > 0)(lambda: own_down(p).wait_send())
            own_side(p).wait_send()
            pl.when(here & (c0 != c))(lambda: own_core(p).wait_send())

        def sent(d):
            def go(zb, more):
                for p in range(HALVES):
                    for cb in range(2):
                        on, side = travel(zb, cb, p, z)
                        pl.when(more)(lambda: on.wait_send())
                        side.wait_send()
            pl.when((z - d >= 0) & (((z - d + lines) // zs_per) % 2 == c))(lambda: go(z - d, z < lines - 1))
            pl.when((z + d < lines) & (((z + d) // zs_per) % 2 == c))(lambda: go(z + d, z > 0))

        @pl.loop(1, lines)
        def _(d):
            sent(d)

    mine, theirs = (1 - x) * 2 + c, (1 - x) * 2 + 1 - c
    if zs_per == 1:
        add([mine], y)
        settle()
        arrived(mine, 1 - y, 0)
        add([mine], 1 - y)
        to_core(1 - x).wait_recv()
        keep(1 - x, 1 - c, mixed_in[1 - x])
        add([theirs], y)
        arrived(theirs, 1 - y, 0)
        add([theirs], 1 - y)
    else:
        to_core(1 - x).wait_recv()
        keep(1 - x, 1 - c, mixed_in[1 - x])
        last_own(y)
        for xb in (x, 1 - x):
            @pl.loop(0, zs_per)
            def _(i):
                others(i, (xb,))
            add([xb * 2, xb * 2 + 1], 0, xb is x)
        settle()

    to_core(1 - x).wait_send()

    @pl.loop(0, zs_per)
    def _(i):
        for p in range(HALVES):
            for cb in range(2):
                over_y(nar * zs_per + i, cb, p).wait_send()


def solution(mesh):
    wides = mesh.shape["wide"]

    def per_device(amplitudes, partner, gate_block, slice_bits, bit_order):
        chosen = choose(partner, slice_bits)
        rows, cols = amplitudes.shape[1:]
        out_bits = gate_block.shape[0]
        low_rows = rows // wides
        block = chosen.shape[0]
        own = block * wides // mesh.shape["narrow"]
        flat = out_bits * low_rows
        smem = pl.BlockSpec(memory_space=pltpu.SMEM)
        vmem = pl.BlockSpec(memory_space=pltpu.VMEM)
        dma = pltpu.SemaphoreType.DMA
        lines = wides // 2
        zs_per = lines // 4
        return pl.pallas_call(
            functools.partial(kernel, wides),
            out_shape=jax.ShapeDtypeStruct((out_bits, low_rows, own), F32),
            in_specs=[smem, smem, vmem, vmem],
            out_specs=vmem,
            scratch_shapes=[
                pltpu.VMEM((wides, low_rows, cols), F32),
                pltpu.VMEM((lines, low_rows, cols), F32),
                pltpu.VMEM((2, wides, low_rows, cols), F32),
                pltpu.VMEM((2, flat, cols), F32),
                pltpu.VMEM((2, flat, cols), F32),
                pltpu.VMEM((4, flat, cols), BF16),
                pltpu.VMEM((4, flat, cols), BF16),
                pltpu.VMEM((6, zs_per * 2, block, cols), F32),
                dma,
                dma((6, zs_per, HALVES)), dma((6, zs_per, HALVES)), dma((zs_per, 2, HALVES)),
                dma((4, HALVES)), dma((6, zs_per * 2, HALVES)),
                dma((wides,)), dma((wides,)), dma((lines,)), dma((lines,)), dma((lines,)), dma((wides,)), dma((wides,)),
                dma((2,)), dma((2,)),
                pltpu.SemaphoreType.REGULAR((lines,)),
            ],
            compiler_params=pltpu.CompilerParams(
                collective_id=0, has_side_effects=True, vmem_limit_bytes=48 * 1024 * 1024),
        )(bit_order, gate_block, amplitudes[0], chosen)

    placed = (P("wide", None, "narrow"), P(None, "wide", "narrow"), P(), P(), P())
    return jax.shard_map(
        per_device, mesh=mesh, in_specs=placed, out_specs=P(None, "wide", "narrow"), check_vma=False
    )
```

```python
import functools

import jax
import jax.numpy as jnp
from jax import lax
from jax.experimental import pallas as pl
from jax.experimental.pallas import tpu as pltpu
from jax.sharding import PartitionSpec as P

F32 = jnp.float32
BF16 = jnp.bfloat16
MESH = pl.DeviceIdType.MESH


def slice_kernel(bits_ref, partner_ref, chosen_ref, sem):
    number = bits_ref[0]
    for j in range(1, bits_ref.shape[0]):
        number = number + bits_ref[j] * (1 << j)
    copy = pltpu.make_async_copy(partner_ref.at[number], chosen_ref, sem)
    copy.start()
    copy.wait()


def choose(partner, slice_bits):
    _, rows, cols = partner.shape
    return pl.pallas_call(
        slice_kernel,
        out_shape=pltpu.VMEM((rows, cols), F32),
        in_specs=[pl.BlockSpec(memory_space=pltpu.SMEM), pl.BlockSpec(memory_space=pl.ANY)],
        out_specs=pl.BlockSpec(memory_space=pltpu.VMEM),
        scratch_shapes=[pltpu.SemaphoreType.DMA],
    )(slice_bits, partner)


def split2(x):
    hi = x.astype(BF16)
    return hi, (x - hi.astype(F32)).astype(BF16)


def dot_nt(a, b):
    return lax.dot_general(a, b, (((1,), (1,)), ((), ())), preferred_element_type=F32)


HALVES = 4

ORDERS = {
    (0, 0, 0): ('BBBBBBBBTTTTThaTTTsssaaaaaampqrn', '1426357', '321'),
    (0, 0, 1): ('IIIIIIIIBBTBhBTaBBTBTBsssTaaTTaaTaampqrn', '1462753', '321'),
    (0, 1, 0): ('aIIIBIBhBIBIBIIBsssaBaBaaaampqrn', '1426357', '321'),
    (0, 1, 1): ('TTTTTTTaTIhIIBIBsssIBaBaIBIaBaaIBamBpqrn', '1465723', '321'),
    (1, 0, 0): ('ITITITITITITITITBBhBBaBBBBsssaaaaaampqrn', '3046157', '302'),
    (1, 0, 1): ('BBBBBBBBTTTTTThTaTsssaaaaaampqrn', '3046517', '302'),
    (1, 1, 0): ('ITITITITIBTITBaIBTITBBBBBhsssaaaaaampqrn', '3046157', '302'),
    (1, 1, 1): ('aIIIIIBIhBIBIBBBBBsssaaaaaampqrn', '3064175', '302'),
}


def tables():
    orders, row_words, stage_words = [], [], []
    for z in range(4):
        for x in range(2):
            for c in range(2):
                flip = z >= 2
                order, rows, stages = ORDERS[(3 - z, 1 - x, 1 - c) if flip else (z, x, c)]
                rows = [(3 - int(r) // 2) * 2 + int(r) % 2 if flip else int(r) for r in rows]
                stages = [3 - int(r) if flip else int(r) for r in stages]
                orders.append([" ITBashmnpqr".index(e) for e in order])
                row_words.append(sum(r * 8 ** k for k, r in enumerate(rows)))
                stage_words.append(sum(r * 4 ** k for k, r in enumerate(stages)))
    length = -(-max(len(o) for o in orders) // 7)
    words = [[sum(e * 16 ** k for k, e in enumerate(o[w * 7:w * 7 + 7])) for o in orders] for w in range(length)]
    return words, row_words, stage_words


def kernel(wides, order_ref, gate_ref, amp_ref, chosen_ref, out_ref,
           send_a, staged, rows_in, mixed, mixed_in, mix_hi, mix_lo, held,
           own_sem, z_send, side_send, y_send, first_send, held_recv,
           a_send, a_recv, st_send, st_recv, sf_send, ax_send, ax_recv, m_send, m_recv, near_sem):
    me = lax.axis_index("wide")
    nar = lax.axis_index("narrow")
    lines = wides // 2
    zs_per = lines // 4
    z, y = me // 2, me % 2
    x, c = nar // 2, nar % 2
    rows, cols = amp_ref.shape
    out_bits, low_rows, wide_cols = out_ref.shape
    block = held.shape[2]
    half = block // HALVES
    flat = out_bits * low_rows

    def dev(zz, yy, xx, cc):
        return (zz * 2 + yy, xx * 2 + cc)

    core_peer = dev(z, y, x, 1 - c)

    def rc(src, dst, ssem, rsem, device):
        return pltpu.make_async_remote_copy(
            src_ref=src, dst_ref=dst, send_sem=ssem, recv_sem=rsem,
            device_id=device, device_id_type=MESH)

    barrier = pltpu.get_barrier_semaphore()

    def greet(device):
        pl.semaphore_signal(barrier, inc=1, device_id=device, device_id_type=MESH)

    def near_z(do):
        pl.when(z > 0)(lambda: do(z - 1))
        pl.when(z < lines - 1)(lambda: do(z + 1))

    greet(core_peer)
    for cc in range(2):
        greet(dev(z, 1 - y, x, cc))
        greet(dev(z, y, 1 - x, cc))
        near_z(lambda zz: greet(dev(zz, y, x, cc)))

    row_ids = lax.broadcasted_iota(jnp.int32, (rows, 128), 0)
    source = jnp.zeros((rows, 128), jnp.int32)
    for j in range(order_ref.shape[0]):
        source = source + (lax.shift_right_logical(row_ids, jnp.broadcast_to(order_ref[j], row_ids.shape)) & 1) * (1 << j)
    lane = lax.broadcasted_iota(jnp.int32, (rows, 128), 1)
    onehot = jnp.concatenate(
        [jnp.where(lane + t * 128 == source, 1.0, 0.0).astype(BF16) for t in range(rows // 128)], axis=1)
    amp = amp_ref[...]
    a1 = amp.astype(BF16)
    rest = amp - a1.astype(F32)
    a2 = rest.astype(BF16)
    a3 = (rest - a2.astype(F32)).astype(BF16)
    moved = (jnp.dot(onehot, a3, preferred_element_type=F32)
             + jnp.dot(onehot, a2, preferred_element_type=F32)
             + jnp.dot(onehot, a1, preferred_element_type=F32))
    send_a[...] = moved.reshape(send_a.shape)

    ends = jnp.where(z > 0, 1, 0) + jnp.where(z < lines - 1, 1, 0)
    pl.semaphore_wait(barrier, 5 + 2 * ends)

    quarter0 = z // zs_per
    x0, c0 = quarter0 // 2, quarter0 % 2
    j0 = (z % zs_per) * 2 + y
    cross0 = (x0 + x) % 2
    slot0 = (1 - cross0) * (2 * x) + cross0 * 4 + c

    def part(p):
        return pl.ds(p * half, half)

    def own(way, device, slot, p):
        return rc(chosen_ref.at[part(p)], held.at[slot, j0, part(p)], first_send.at[way, p], held_recv.at[slot, j0, p], device)

    def own_up(p):
        return own(0, dev((z + 1) % lines, y, x, c0), slot0, p)

    def own_down(p):
        return own(1, dev((z + lines - 1) % lines, y, x, c0), slot0, p)

    def own_side(p):
        return own(2, dev(z, (y + 1 - cross0) % 2, (x + cross0) % 2, c0), x * 2 + c, p)

    def own_core(p):
        return own(3, core_peer, x * 2 + c, p)

    own_copy = pltpu.make_async_copy(chosen_ref, held.at[x * 2 + c, j0], own_sem)
    here = cross0 == 0
    rows_in[x, me] = send_a[me]

    def a_out(zz, yy):
        to = zz * 2 + yy
        return rc(send_a.at[to], rows_in.at[x, me], a_send.at[to], a_recv.at[me], (to, nar))

    def a_in(frm):
        return rc(send_a.at[frm], rows_in.at[x, frm], a_send.at[frm], a_recv.at[frm], (frm, nar))

    def stage(zz):
        return rc(send_a.at[zz * 2 + 1 - y], staged.at[zz], st_send.at[zz], st_recv.at[zz], dev(z, 1 - y, x, c))

    def stage_on(zz):
        frm = z * 2 + 1 - y
        return rc(staged.at[zz], rows_in.at[x, frm], sf_send.at[zz], a_recv.at[frm], dev(zz, y, x, c))

    def ax_out(h):
        return rc(rows_in.at[x, h], rows_in.at[x, h], ax_send.at[h], ax_recv.at[h], dev(z, y, 1 - x, c))

    def ax_in(h):
        return rc(rows_in.at[1 - x, h], rows_in.at[1 - x, h], ax_send.at[h], ax_recv.at[h], dev(z, y, 1 - x, c))

    def line(d, do):
        pl.when(z - d >= 0)(lambda: do(z - d))
        pl.when(z + d < lines)(lambda: do(z + d))

    def each_line(do):
        if lines == 4:
            for d in range(lines - 1, 0, -1):
                line(d, do)
        else:
            @pl.loop(1, lines)
            def _(d):
                line(d, do)

    def send_stage():
        each_line(lambda zz: stage(zz).start())
        a_out(z, 1 - y).start()

    pl.when(cross0 == 1)(send_stage)
    for p in range(HALVES):
        pl.when(z < lines - 1)(lambda: own_up(p).start())
        pl.when(z > 0)(lambda: own_down(p).start())
        own_side(p).start()
    pl.when(here)(send_stage)
    ax_out(me).start()

    @pl.when(here & (c0 != c))
    def _():
        for p in range(HALVES):
            own_core(p).start()

    @pl.when(here & (c0 == c))
    def _():
        own_copy.start()

    def tell(r):
        near_z(lambda zz: pl.semaphore_signal(
            near_sem.at[r - 2], inc=1, device_id=dev(zz, y, x, c), device_id_type=MESH))

    def heard(r):
        pl.semaphore_wait(near_sem.at[r - 2], ends)

    def forward_stage():
        def one(zz):
            stage(zz).wait_recv()
            stage_on(zz).start()
        each_line(one)

    def pass_one(zz, yy):
        h = zz * 2 + yy
        a_in(h).wait_recv()
        ax_out(h).start()

    def pass_rows(d):
        line(d, lambda zz: pass_one(zz, y))
        line(d, lambda zz: pass_one(zz, 1 - y))

    def travel(zb, cb, p, to_z):
        q = zb // zs_per
        cross = (q // 2 + x) % 2
        i = zb % zs_per
        slot = (1 - cross) * (2 * x) + cross * 4 + cb
        src = held.at[slot, i * 2 + y, part(p)]
        on = rc(src, src, z_send.at[slot, i, p], held_recv.at[slot, i * 2 + y, p], dev(to_z % lines, y, x, c))
        side = rc(src, held.at[x * 2 + cb, i * 2 + y, part(p)], side_send.at[slot, i, p],
                  held_recv.at[x * 2 + cb, i * 2 + y, p],
                  dev(z, (y + 1 - cross) % 2, (x + cross) % 2, c))
        return on, side

    def take(zb, cb, p, to_z, more):
        on, side = travel(zb, cb, p, to_z)
        on.wait_recv()
        pl.when(more)(lambda: on.start())
        side.start()

    def line_step(d):
        def go(zb, to_z, more):
            for p in range(HALVES):
                for cb in range(2):
                    take(zb, cb, p, to_z, more)
        pl.when((z - d >= 0) & (((z - d + lines) // zs_per) % 2 == c))(lambda: go(z - d, z + 1, z < lines - 1))
        pl.when((z + d < lines) & (((z + d) // zs_per) % 2 == c))(lambda: go(z + d, z - 1 + lines, z > 0))

    def over_y(zb, cb, p):
        i = zb % zs_per
        slot = (1 - x) * 2 + cb
        src = held.at[slot, i * 2 + y, part(p)]
        return rc(src, src, y_send.at[i, cb, p], held_recv.at[slot, i * 2 + y, p], dev(z, 1 - y, x, c))

    def take_x(zb, cb, p):
        copy = over_y(zb, cb, p)
        copy.wait_recv()
        copy.start()

    def x_step(d):
        def go(zb):
            for p in range(HALVES):
                for cb in range(2):
                    take_x(zb, cb, p)
        pl.when((z - d >= 0) & ((z - d + lines) // zs_per == nar + 4))(lambda: go(z - d))
        if not (isinstance(d, int) and d == 0):
            pl.when((z + d < lines) & ((z + d) // zs_per == nar))(lambda: go(z + d))

    def mix(xb):
        @pl.loop(0, out_bits)
        def _(q):
            acc = gate_ref[q, 0] * rows_in[xb, 0]
            for h in range(1, wides):
                acc = acc + gate_ref[q, h] * rows_in[xb, h]
            mixed[xb, pl.ds(pl.multiple_of(q * low_rows, 8), low_rows)] = acc

    def to_core(xb):
        return rc(mixed.at[xb], mixed_in.at[xb], m_send.at[xb], m_recv.at[xb], core_peer)

    def keep(xb, cc, value):
        hi, lo = split2(value)
        mix_hi[xb * 2 + cc] = hi
        mix_lo[xb * 2 + cc] = lo

    def arrived(slot, yb, i):
        for p in range(HALVES):
            src = held.at[slot, i * 2 + yb, part(p)]
            rc(src, src, y_send.at[i, 0, p], held_recv.at[slot, i * 2 + yb, p], core_peer).wait_recv()

    def both(slots, b):
        left, right = [], []
        for slot, value in zip(slots, b):
            bh, bl = split2(value)
            mh, ml = mix_hi[slot], mix_lo[slot]
            left += [mh, ml, mh]
            right += [bl, bh, bh]
        return dot_nt(jnp.concatenate(left, axis=1), jnp.concatenate(right, axis=1))

    def put(at_n, value, first):
        value = value.reshape(out_bits, low_rows, value.shape[1])
        if first:
            out_ref[:, :, at_n] = value
        else:
            out_ref[:, :, at_n] = out_ref[:, :, at_n] + value

    def add(slots, yb, first=False):
        if zs_per == 1:
            at_n = pl.ds(pl.multiple_of(yb * block, 128), block)
            put(at_n, both(slots, [held[slot, yb] for slot in slots]), first)
        else:
            put(slice(None), both(slots, [held[slot].reshape(wide_cols, cols) for slot in slots]), first)

    def add_two(xb, yb, first=False):
        if isinstance(first, bool) and first:
            last_own(yb)
        slots = [xb * 2, xb * 2 + 1]
        if yb is not y:
            for slot in slots:
                arrived(slot, yb, 0)
        add(slots, yb, first)

    def last_own(yb):
        if yb is y:
            @pl.when(here & (c0 == c))
            def _():
                own_copy.wait()
                arrived(x * 2 + 1 - c, y, z % zs_per)

    def others(i, slots):
        for xb in slots:
            for cb in range(2):
                arrived(xb * 2 + cb, 1 - y, i)

    def mix_near():
        mix(x)
        to_core(x).start()
        keep(x, c, mixed[x])

    def swap_near():
        to_core(x).wait_recv()
        keep(x, 1 - c, mixed_in[x])

    def mix_far():
        ax_in(me).wait_recv()

        @pl.loop(1, wides)
        def _(s):
            ax_in((me + s) % wides).wait_recv()
        mix(1 - x)
        to_core(1 - x).start()
        keep(1 - x, c, mixed[1 - x])

    tell(2)
    heard(2)
    if lines == 4:
        tell(3)
        place = z * 4 + x * 2 + c
        words, rows_word, stage_word = tables()

        def pick(values):
            if len(set(values)) == 1:
                return jnp.int32(values[0])
            word = jnp.int32(values[0])
            for k in range(1, len(values)):
                word = jnp.where(place == k, values[k], word)
            return word

        steps = [pick(v) for v in words]
        other = (1 - x) * 2 + c

        def passing(zb, n):
            below = zb < z
            take(zb, n % 2, n // 2, jnp.where(below, z + 1, z + 3), jnp.where(below, z < lines - 1, z > 0))

        def event(_, carry):
            word, ni, nt, nb, a_word, s_word = carry
            kind = word % 16

            @pl.when(kind < 4)
            def _():
                @pl.when(kind == 1)
                def _():
                    passing(nar, ni)

                @pl.when(kind == 2)
                def _():
                    passing(other, nt)

                @pl.when(kind == 3)
                def _():
                    take_x(nar, nb % 2, nb // 2)

            @pl.when((kind >= 4) & (kind < 7))
            def _():
                @pl.when(kind == 4)
                def _():
                    pass_one(a_word % 8 // 2, (y + a_word) % 2)

                @pl.when(kind == 5)
                def _():
                    zz = s_word % 4
                    stage(zz).wait_recv()
                    stage_on(zz).start()

                @pl.when(kind == 6)
                def _():
                    heard(3)
                    each_line(lambda zz: a_out(zz, y).start())

            @pl.when(kind >= 7)
            def _():
                pl.when(kind == 7)(mix_near)
                pl.when(kind == 8)(mix_far)
                pl.when(kind == 9)(swap_near)
                pl.when(kind == 10)(lambda: add_two(x, y, True))
                pl.when(kind == 11)(lambda: add_two(x, 1 - y, True))
            one = lambda k: jnp.where(kind == k, 1, 0)
            return (word // 16, ni + one(1), nt + one(2), nb + one(3),
                    jnp.where(kind == 4, a_word // 8, a_word), jnp.where(kind == 5, s_word // 4, s_word))

        def stretch(w, carry):
            word = steps[0]
            for k in range(1, len(steps)):
                word = jnp.where(w == k, steps[k], word)
            return lax.fori_loop(0, 7, event, (word, *carry))[1:]

        zero = jnp.int32(0)
        lax.fori_loop(0, len(steps), stretch, (zero, zero, zero, pick(rows_word), pick(stage_word)))
    else:
        @pl.loop(3, lines)
        def _(r):
            tell(r)
            heard(r)

        x_step(0)
        each_line(lambda zz: a_out(zz, y).start())
        forward_stage()

        @pl.loop(1, lines)
        def _(d):
            line_step(d)
            x_step(d)
        pass_one(z, 1 - y)

        @pl.loop(1, lines)
        def _(d):
            pass_rows(d)
        mix_near()
        mix_far()
        swap_near()
    def settle():
        to_core(x).wait_send()

        @pl.loop(0, wides)
        def _(h):
            ax_out(h).wait_send()

        a_out(z, 1 - y).wait_send()

        @pl.loop(1, lines)
        def _(s):
            zz = (z + s) % lines
            a_out(zz, y).wait_send()
            stage(zz).wait_send()
            stage_on(zz).wait_send()
        for p in range(HALVES):
            pl.when(z < lines - 1)(lambda: own_up(p).wait_send())
            pl.when(z > 0)(lambda: own_down(p).wait_send())
            own_side(p).wait_send()
            pl.when(here & (c0 != c))(lambda: own_core(p).wait_send())

        def sent(d):
            def go(zb, more):
                for p in range(HALVES):
                    for cb in range(2):
                        on, side = travel(zb, cb, p, z)
                        pl.when(more)(lambda: on.wait_send())
                        side.wait_send()
            pl.when((z - d >= 0) & (((z - d + lines) // zs_per) % 2 == c))(lambda: go(z - d, z < lines - 1))
            pl.when((z + d < lines) & (((z + d) // zs_per) % 2 == c))(lambda: go(z + d, z > 0))

        @pl.loop(1, lines)
        def _(d):
            sent(d)

    mine, theirs = (1 - x) * 2 + c, (1 - x) * 2 + 1 - c
    if zs_per == 1:
        add([mine], y)
        settle()
        arrived(mine, 1 - y, 0)
        add([mine], 1 - y)
        to_core(1 - x).wait_recv()
        keep(1 - x, 1 - c, mixed_in[1 - x])
        add([theirs], y)
        arrived(theirs, 1 - y, 0)
        add([theirs], 1 - y)
    else:
        to_core(1 - x).wait_recv()
        keep(1 - x, 1 - c, mixed_in[1 - x])
        last_own(y)
        for xb in (x, 1 - x):
            @pl.loop(0, zs_per)
            def _(i):
                others(i, (xb,))
            add([xb * 2, xb * 2 + 1], 0, xb is x)
        settle()

    to_core(1 - x).wait_send()

    @pl.loop(0, zs_per)
    def _(i):
        for p in range(HALVES):
            for cb in range(2):
                over_y(nar * zs_per + i, cb, p).wait_send()


def solution(mesh):
    wides = mesh.shape["wide"]

    def per_device(amplitudes, partner, gate_block, slice_bits, bit_order):
        chosen = choose(partner, slice_bits)
        rows, cols = amplitudes.shape[1:]
        out_bits = gate_block.shape[0]
        low_rows = rows // wides
        block = chosen.shape[0]
        own = block * wides // mesh.shape["narrow"]
        flat = out_bits * low_rows
        smem = pl.BlockSpec(memory_space=pltpu.SMEM)
        vmem = pl.BlockSpec(memory_space=pltpu.VMEM)
        dma = pltpu.SemaphoreType.DMA
        lines = wides // 2
        zs_per = lines // 4
        return pl.pallas_call(
            functools.partial(kernel, wides),
            out_shape=jax.ShapeDtypeStruct((out_bits, low_rows, own), F32),
            in_specs=[smem, smem, vmem, vmem],
            out_specs=vmem,
            scratch_shapes=[
                pltpu.VMEM((wides, low_rows, cols), F32),
                pltpu.VMEM((lines, low_rows, cols), F32),
                pltpu.VMEM((2, wides, low_rows, cols), F32),
                pltpu.VMEM((2, flat, cols), F32),
                pltpu.VMEM((2, flat, cols), F32),
                pltpu.VMEM((4, flat, cols), BF16),
                pltpu.VMEM((4, flat, cols), BF16),
                pltpu.VMEM((6, zs_per * 2, block, cols), F32),
                dma,
                dma((6, zs_per, HALVES)), dma((6, zs_per, HALVES)), dma((zs_per, 2, HALVES)),
                dma((4, HALVES)), dma((6, zs_per * 2, HALVES)),
                dma((wides,)), dma((wides,)), dma((lines,)), dma((lines,)), dma((lines,)), dma((wides,)), dma((wides,)),
                dma((2,)), dma((2,)),
                pltpu.SemaphoreType.REGULAR((lines,)),
            ],
            compiler_params=pltpu.CompilerParams(
                collective_id=0, has_side_effects=True, vmem_limit_bytes=48 * 1024 * 1024),
        )(bit_order, gate_block, amplitudes[0], chosen)

    placed = (P("wide", None, "narrow"), P(None, "wide", "narrow"), P(), P(), P())
    return jax.shard_map(
        per_device, mesh=mesh, in_specs=placed, out_specs=P(None, "wide", "narrow"), check_vma=False
    )
```

```python
import functools

import jax
import jax.numpy as jnp
from jax import lax
from jax.experimental import pallas as pl
from jax.experimental.pallas import tpu as pltpu
from jax.sharding import PartitionSpec as P

F32 = jnp.float32
BF16 = jnp.bfloat16
MESH = pl.DeviceIdType.MESH


def slice_kernel(bits_ref, partner_ref, chosen_ref, sem):
    number = bits_ref[0]
    for j in range(1, bits_ref.shape[0]):
        number = number + bits_ref[j] * (1 << j)
    copy = pltpu.make_async_copy(partner_ref.at[number], chosen_ref, sem)
    copy.start()
    copy.wait()


def choose(partner, slice_bits):
    _, rows, cols = partner.shape
    return pl.pallas_call(
        slice_kernel,
        out_shape=pltpu.VMEM((rows, cols), F32),
        in_specs=[pl.BlockSpec(memory_space=pltpu.SMEM), pl.BlockSpec(memory_space=pl.ANY)],
        out_specs=pl.BlockSpec(memory_space=pltpu.VMEM),
        scratch_shapes=[pltpu.SemaphoreType.DMA],
    )(slice_bits, partner)


def split2(x):
    hi = x.astype(BF16)
    return hi, (x - hi.astype(F32)).astype(BF16)


def dot_nt(a, b):
    return lax.dot_general(a, b, (((1,), (1,)), ((), ())), preferred_element_type=F32)


HALVES = 4

ORDERS = {
    (0, 0, 0): ('BBBBBBBBTTTTThaTTTsssaaaaaampqrn', '1246357', '321'),
    (0, 0, 1): ('IIIIIIIIBBThBBTaBBTBTBsssaTaTaTaaTampqrn', '1465723', '321'),
    (0, 1, 0): ('aIIIBIBhBIBIBIIBsssBaBaaaaampqrn', '1426357', '321'),
    (0, 1, 1): ('TTTTTTTaTIhIIBIBsssIBaBaIBIaaaBIamBpqBrn', '1465723', '321'),
    (1, 0, 0): ('ITITITITITITITITBBhBBaBBBBsssaaaaaampqrn', '3046175', '302'),
    (1, 0, 1): ('BBBBBBBBTTTTThTTaTsssaaaaaampqrn', '3046157', '302'),
    (1, 1, 0): ('ITITITITIBTITBaIBTITBBBBBhsssaaaaaampqrn', '3046157', '302'),
    (1, 1, 1): ('aIIIIIBIhBIBIBBBBBsssaaaaaampqrn', '3064175', '302'),
}


def tables():
    orders, row_words, stage_words = [], [], []
    for z in range(4):
        for x in range(2):
            for c in range(2):
                flip = z >= 2
                order, rows, stages = ORDERS[(3 - z, 1 - x, 1 - c) if flip else (z, x, c)]
                rows = [(3 - int(r) // 2) * 2 + int(r) % 2 if flip else int(r) for r in rows]
                stages = [3 - int(r) if flip else int(r) for r in stages]
                orders.append([" ITBashmnpqr".index(e) for e in order])
                row_words.append(sum(r * 8 ** k for k, r in enumerate(rows)))
                stage_words.append(sum(r * 4 ** k for k, r in enumerate(stages)))
    length = -(-max(len(o) for o in orders) // 7)
    words = [[sum(e * 16 ** k for k, e in enumerate(o[w * 7:w * 7 + 7])) for o in orders] for w in range(length)]
    return words, row_words, stage_words


def kernel(wides, order_ref, gate_ref, amp_ref, chosen_ref, out_ref,
           send_a, staged, rows_in, mixed, mixed_in, mix_hi, mix_lo, held,
           own_sem, z_send, side_send, y_send, first_send, held_recv,
           a_send, a_recv, st_send, st_recv, sf_send, ax_send, ax_recv, m_send, m_recv, near_sem):
    me = lax.axis_index("wide")
    nar = lax.axis_index("narrow")
    lines = wides // 2
    zs_per = lines // 4
    z, y = me // 2, me % 2
    x, c = nar // 2, nar % 2
    rows, cols = amp_ref.shape
    out_bits, low_rows, wide_cols = out_ref.shape
    block = held.shape[2]
    half = block // HALVES
    flat = out_bits * low_rows

    def dev(zz, yy, xx, cc):
        return (zz * 2 + yy, xx * 2 + cc)

    core_peer = dev(z, y, x, 1 - c)

    def rc(src, dst, ssem, rsem, device):
        return pltpu.make_async_remote_copy(
            src_ref=src, dst_ref=dst, send_sem=ssem, recv_sem=rsem,
            device_id=device, device_id_type=MESH)

    barrier = pltpu.get_barrier_semaphore()

    def greet(device):
        pl.semaphore_signal(barrier, inc=1, device_id=device, device_id_type=MESH)

    def near_z(do):
        pl.when(z > 0)(lambda: do(z - 1))
        pl.when(z < lines - 1)(lambda: do(z + 1))

    greet(core_peer)
    for cc in range(2):
        greet(dev(z, 1 - y, x, cc))
        greet(dev(z, y, 1 - x, cc))
        near_z(lambda zz: greet(dev(zz, y, x, cc)))

    row_ids = lax.broadcasted_iota(jnp.int32, (rows, 128), 0)
    source = jnp.zeros((rows, 128), jnp.int32)
    for j in range(order_ref.shape[0]):
        source = source + (lax.shift_right_logical(row_ids, jnp.broadcast_to(order_ref[j], row_ids.shape)) & 1) * (1 << j)
    lane = lax.broadcasted_iota(jnp.int32, (rows, 128), 1)
    onehot = jnp.concatenate(
        [jnp.where(lane + t * 128 == source, 1.0, 0.0).astype(BF16) for t in range(rows // 128)], axis=1)
    amp = amp_ref[...]
    a1 = amp.astype(BF16)
    rest = amp - a1.astype(F32)
    a2 = rest.astype(BF16)
    a3 = (rest - a2.astype(F32)).astype(BF16)
    moved = (jnp.dot(onehot, a3, preferred_element_type=F32)
             + jnp.dot(onehot, a2, preferred_element_type=F32)
             + jnp.dot(onehot, a1, preferred_element_type=F32))
    send_a[...] = moved.reshape(send_a.shape)

    ends = jnp.where(z > 0, 1, 0) + jnp.where(z < lines - 1, 1, 0)
    pl.semaphore_wait(barrier, 5 + 2 * ends)

    quarter0 = z // zs_per
    x0, c0 = quarter0 // 2, quarter0 % 2
    j0 = (z % zs_per) * 2 + y
    cross0 = (x0 + x) % 2
    slot0 = (1 - cross0) * (2 * x) + cross0 * 4 + c

    def part(p):
        return pl.ds(p * half, half)

    def own(way, device, slot, p):
        return rc(chosen_ref.at[part(p)], held.at[slot, j0, part(p)], first_send.at[way, p], held_recv.at[slot, j0, p], device)

    def own_up(p):
        return own(0, dev((z + 1) % lines, y, x, c0), slot0, p)

    def own_down(p):
        return own(1, dev((z + lines - 1) % lines, y, x, c0), slot0, p)

    def own_side(p):
        return own(2, dev(z, (y + 1 - cross0) % 2, (x + cross0) % 2, c0), x * 2 + c, p)

    def own_core(p):
        return own(3, core_peer, x * 2 + c, p)

    own_copy = pltpu.make_async_copy(chosen_ref, held.at[x * 2 + c, j0], own_sem)
    here = cross0 == 0
    rows_in[x, me] = send_a[me]

    def a_out(zz, yy):
        to = zz * 2 + yy
        return rc(send_a.at[to], rows_in.at[x, me], a_send.at[to], a_recv.at[me], (to, nar))

    def a_in(frm):
        return rc(send_a.at[frm], rows_in.at[x, frm], a_send.at[frm], a_recv.at[frm], (frm, nar))

    def stage(zz):
        return rc(send_a.at[zz * 2 + 1 - y], staged.at[zz], st_send.at[zz], st_recv.at[zz], dev(z, 1 - y, x, c))

    def stage_on(zz):
        frm = z * 2 + 1 - y
        return rc(staged.at[zz], rows_in.at[x, frm], sf_send.at[zz], a_recv.at[frm], dev(zz, y, x, c))

    def ax_out(h):
        return rc(rows_in.at[x, h], rows_in.at[x, h], ax_send.at[h], ax_recv.at[h], dev(z, y, 1 - x, c))

    def ax_in(h):
        return rc(rows_in.at[1 - x, h], rows_in.at[1 - x, h], ax_send.at[h], ax_recv.at[h], dev(z, y, 1 - x, c))

    def line(d, do):
        pl.when(z - d >= 0)(lambda: do(z - d))
        pl.when(z + d < lines)(lambda: do(z + d))

    def each_line(do):
        if lines == 4:
            for d in range(lines - 1, 0, -1):
                line(d, do)
        else:
            @pl.loop(1, lines)
            def _(d):
                line(d, do)

    def send_stage():
        each_line(lambda zz: stage(zz).start())
        a_out(z, 1 - y).start()

    pl.when(cross0 == 1)(send_stage)
    for p in range(HALVES):
        pl.when(z < lines - 1)(lambda: own_up(p).start())
        pl.when(z > 0)(lambda: own_down(p).start())
        own_side(p).start()
    pl.when(here)(send_stage)
    ax_out(me).start()

    @pl.when(here & (c0 != c))
    def _():
        for p in range(HALVES):
            own_core(p).start()

    @pl.when(here & (c0 == c))
    def _():
        own_copy.start()

    def tell(r):
        near_z(lambda zz: pl.semaphore_signal(
            near_sem.at[r - 2], inc=1, device_id=dev(zz, y, x, c), device_id_type=MESH))

    def heard(r):
        pl.semaphore_wait(near_sem.at[r - 2], ends)

    def forward_stage():
        def one(zz):
            stage(zz).wait_recv()
            stage_on(zz).start()
        each_line(one)

    def pass_one(zz, yy):
        h = zz * 2 + yy
        a_in(h).wait_recv()
        ax_out(h).start()

    def pass_rows(d):
        line(d, lambda zz: pass_one(zz, y))
        line(d, lambda zz: pass_one(zz, 1 - y))

    def travel(zb, cb, p, to_z):
        q = zb // zs_per
        cross = (q // 2 + x) % 2
        i = zb % zs_per
        slot = (1 - cross) * (2 * x) + cross * 4 + cb
        src = held.at[slot, i * 2 + y, part(p)]
        on = rc(src, src, z_send.at[slot, i, p], held_recv.at[slot, i * 2 + y, p], dev(to_z % lines, y, x, c))
        side = rc(src, held.at[x * 2 + cb, i * 2 + y, part(p)], side_send.at[slot, i, p],
                  held_recv.at[x * 2 + cb, i * 2 + y, p],
                  dev(z, (y + 1 - cross) % 2, (x + cross) % 2, c))
        return on, side

    def take(zb, cb, p, to_z, more):
        on, side = travel(zb, cb, p, to_z)
        on.wait_recv()
        pl.when(more)(lambda: on.start())
        side.start()

    def line_step(d):
        def go(zb, to_z, more):
            for p in range(HALVES):
                for cb in range(2):
                    take(zb, cb, p, to_z, more)
        pl.when((z - d >= 0) & (((z - d + lines) // zs_per) % 2 == c))(lambda: go(z - d, z + 1, z < lines - 1))
        pl.when((z + d < lines) & (((z + d) // zs_per) % 2 == c))(lambda: go(z + d, z - 1 + lines, z > 0))

    def over_y(zb, cb, p):
        i = zb % zs_per
        slot = (1 - x) * 2 + cb
        src = held.at[slot, i * 2 + y, part(p)]
        return rc(src, src, y_send.at[i, cb, p], held_recv.at[slot, i * 2 + y, p], dev(z, 1 - y, x, c))

    def take_x(zb, cb, p):
        copy = over_y(zb, cb, p)
        copy.wait_recv()
        copy.start()

    def x_step(d):
        def go(zb):
            for p in range(HALVES):
                for cb in range(2):
                    take_x(zb, cb, p)
        pl.when((z - d >= 0) & ((z - d + lines) // zs_per == nar + 4))(lambda: go(z - d))
        if not (isinstance(d, int) and d == 0):
            pl.when((z + d < lines) & ((z + d) // zs_per == nar))(lambda: go(z + d))

    def mix(xb):
        @pl.loop(0, out_bits)
        def _(q):
            acc = gate_ref[q, 0] * rows_in[xb, 0]
            for h in range(1, wides):
                acc = acc + gate_ref[q, h] * rows_in[xb, h]
            mixed[xb, pl.ds(pl.multiple_of(q * low_rows, 8), low_rows)] = acc

    def to_core(xb):
        return rc(mixed.at[xb], mixed_in.at[xb], m_send.at[xb], m_recv.at[xb], core_peer)

    def keep(xb, cc, value):
        hi, lo = split2(value)
        mix_hi[xb * 2 + cc] = hi
        mix_lo[xb * 2 + cc] = lo

    def arrived(slot, yb, i):
        for p in range(HALVES):
            src = held.at[slot, i * 2 + yb, part(p)]
            rc(src, src, y_send.at[i, 0, p], held_recv.at[slot, i * 2 + yb, p], core_peer).wait_recv()

    def both(slots, b):
        left, right = [], []
        for slot, value in zip(slots, b):
            bh, bl = split2(value)
            mh, ml = mix_hi[slot], mix_lo[slot]
            left += [mh, ml, mh]
            right += [bl, bh, bh]
        return dot_nt(jnp.concatenate(left, axis=1), jnp.concatenate(right, axis=1))

    def put(at_n, value, first):
        value = value.reshape(out_bits, low_rows, value.shape[1])
        if first:
            out_ref[:, :, at_n] = value
        else:
            out_ref[:, :, at_n] = out_ref[:, :, at_n] + value

    def add(slots, yb, first=False):
        if zs_per == 1:
            at_n = pl.ds(pl.multiple_of(yb * block, 128), block)
            put(at_n, both(slots, [held[slot, yb] for slot in slots]), first)
        else:
            put(slice(None), both(slots, [held[slot].reshape(wide_cols, cols) for slot in slots]), first)

    def add_two(xb, yb, first=False):
        if isinstance(first, bool) and first:
            last_own(yb)
        slots = [xb * 2, xb * 2 + 1]
        if yb is not y:
            for slot in slots:
                arrived(slot, yb, 0)
        add(slots, yb, first)

    def last_own(yb):
        if yb is y:
            @pl.when(here & (c0 == c))
            def _():
                own_copy.wait()
                arrived(x * 2 + 1 - c, y, z % zs_per)

    def others(i, slots):
        for xb in slots:
            for cb in range(2):
                arrived(xb * 2 + cb, 1 - y, i)

    def mix_near():
        mix(x)
        to_core(x).start()
        keep(x, c, mixed[x])

    def swap_near():
        to_core(x).wait_recv()
        keep(x, 1 - c, mixed_in[x])

    def mix_far():
        ax_in(me).wait_recv()

        @pl.loop(1, wides)
        def _(s):
            ax_in((me + s) % wides).wait_recv()
        mix(1 - x)
        to_core(1 - x).start()
        keep(1 - x, c, mixed[1 - x])

    tell(2)
    heard(2)
    if lines == 4:
        tell(3)
        place = z * 4 + x * 2 + c
        words, rows_word, stage_word = tables()

        def pick(values):
            if len(set(values)) == 1:
                return jnp.int32(values[0])
            word = jnp.int32(values[0])
            for k in range(1, len(values)):
                word = jnp.where(place == k, values[k], word)
            return word

        steps = [pick(v) for v in words]
        other = (1 - x) * 2 + c

        def passing(zb, n):
            below = zb < z
            take(zb, n % 2, n // 2, jnp.where(below, z + 1, z + 3), jnp.where(below, z < lines - 1, z > 0))

        def event(_, carry):
            word, ni, nt, nb, a_word, s_word = carry
            kind = word % 16

            @pl.when(kind < 4)
            def _():
                @pl.when(kind == 1)
                def _():
                    passing(nar, ni)

                @pl.when(kind == 2)
                def _():
                    passing(other, nt)

                @pl.when(kind == 3)
                def _():
                    take_x(nar, nb % 2, nb // 2)

            @pl.when((kind >= 4) & (kind < 7))
            def _():
                @pl.when(kind == 4)
                def _():
                    pass_one(a_word % 8 // 2, (y + a_word) % 2)

                @pl.when(kind == 5)
                def _():
                    zz = s_word % 4
                    stage(zz).wait_recv()
                    stage_on(zz).start()

                @pl.when(kind == 6)
                def _():
                    heard(3)
                    each_line(lambda zz: a_out(zz, y).start())

            @pl.when(kind >= 7)
            def _():
                pl.when(kind == 7)(mix_near)
                pl.when(kind == 8)(mix_far)
                pl.when(kind == 9)(swap_near)
                pl.when(kind == 10)(lambda: add_two(x, y, True))
                pl.when(kind == 11)(lambda: add_two(x, 1 - y, True))
            one = lambda k: jnp.where(kind == k, 1, 0)
            return (word // 16, ni + one(1), nt + one(2), nb + one(3),
                    jnp.where(kind == 4, a_word // 8, a_word), jnp.where(kind == 5, s_word // 4, s_word))

        def stretch(w, carry):
            word = steps[0]
            for k in range(1, len(steps)):
                word = jnp.where(w == k, steps[k], word)
            return lax.fori_loop(0, 7, event, (word, *carry))[1:]

        zero = jnp.int32(0)
        lax.fori_loop(0, len(steps), stretch, (zero, zero, zero, pick(rows_word), pick(stage_word)))
    else:
        @pl.loop(3, lines)
        def _(r):
            tell(r)
            heard(r)

        x_step(0)
        each_line(lambda zz: a_out(zz, y).start())
        forward_stage()

        @pl.loop(1, lines)
        def _(d):
            line_step(d)
            x_step(d)
        pass_one(z, 1 - y)

        @pl.loop(1, lines)
        def _(d):
            pass_rows(d)
        mix_near()
        mix_far()
        swap_near()
    def settle():
        to_core(x).wait_send()

        @pl.loop(0, wides)
        def _(h):
            ax_out(h).wait_send()

        a_out(z, 1 - y).wait_send()

        @pl.loop(1, lines)
        def _(s):
            zz = (z + s) % lines
            a_out(zz, y).wait_send()
            stage(zz).wait_send()
            stage_on(zz).wait_send()
        for p in range(HALVES):
            pl.when(z < lines - 1)(lambda: own_up(p).wait_send())
            pl.when(z > 0)(lambda: own_down(p).wait_send())
            own_side(p).wait_send()
            pl.when(here & (c0 != c))(lambda: own_core(p).wait_send())

        def sent(d):
            def go(zb, more):
                for p in range(HALVES):
                    for cb in range(2):
                        on, side = travel(zb, cb, p, z)
                        pl.when(more)(lambda: on.wait_send())
                        side.wait_send()
            pl.when((z - d >= 0) & (((z - d + lines) // zs_per) % 2 == c))(lambda: go(z - d, z < lines - 1))
            pl.when((z + d < lines) & (((z + d) // zs_per) % 2 == c))(lambda: go(z + d, z > 0))

        @pl.loop(1, lines)
        def _(d):
            sent(d)

    mine, theirs = (1 - x) * 2 + c, (1 - x) * 2 + 1 - c
    if zs_per == 1:
        add([mine], y)
        settle()
        arrived(mine, 1 - y, 0)
        add([mine], 1 - y)
        to_core(1 - x).wait_recv()
        keep(1 - x, 1 - c, mixed_in[1 - x])
        add([theirs], y)
        arrived(theirs, 1 - y, 0)
        add([theirs], 1 - y)
    else:
        to_core(1 - x).wait_recv()
        keep(1 - x, 1 - c, mixed_in[1 - x])
        last_own(y)
        for xb in (x, 1 - x):
            @pl.loop(0, zs_per)
            def _(i):
                others(i, (xb,))
            add([xb * 2, xb * 2 + 1], 0, xb is x)
        settle()

    to_core(1 - x).wait_send()

    @pl.loop(0, zs_per)
    def _(i):
        for p in range(HALVES):
            for cb in range(2):
                over_y(nar * zs_per + i, cb, p).wait_send()


def solution(mesh):
    wides = mesh.shape["wide"]

    def per_device(amplitudes, partner, gate_block, slice_bits, bit_order):
        chosen = choose(partner, slice_bits)
        rows, cols = amplitudes.shape[1:]
        out_bits = gate_block.shape[0]
        low_rows = rows // wides
        block = chosen.shape[0]
        own = block * wides // mesh.shape["narrow"]
        flat = out_bits * low_rows
        smem = pl.BlockSpec(memory_space=pltpu.SMEM)
        vmem = pl.BlockSpec(memory_space=pltpu.VMEM)
        dma = pltpu.SemaphoreType.DMA
        lines = wides // 2
        zs_per = lines // 4
        return pl.pallas_call(
            functools.partial(kernel, wides),
            out_shape=jax.ShapeDtypeStruct((out_bits, low_rows, own), F32),
            in_specs=[smem, smem, vmem, vmem],
            out_specs=vmem,
            scratch_shapes=[
                pltpu.VMEM((wides, low_rows, cols), F32),
                pltpu.VMEM((lines, low_rows, cols), F32),
                pltpu.VMEM((2, wides, low_rows, cols), F32),
                pltpu.VMEM((2, flat, cols), F32),
                pltpu.VMEM((2, flat, cols), F32),
                pltpu.VMEM((4, flat, cols), BF16),
                pltpu.VMEM((4, flat, cols), BF16),
                pltpu.VMEM((6, zs_per * 2, block, cols), F32),
                dma,
                dma((6, zs_per, HALVES)), dma((6, zs_per, HALVES)), dma((zs_per, 2, HALVES)),
                dma((4, HALVES)), dma((6, zs_per * 2, HALVES)),
                dma((wides,)), dma((wides,)), dma((lines,)), dma((lines,)), dma((lines,)), dma((wides,)), dma((wides,)),
                dma((2,)), dma((2,)),
                pltpu.SemaphoreType.REGULAR((lines,)),
            ],
            compiler_params=pltpu.CompilerParams(
                collective_id=0, has_side_effects=True, vmem_limit_bytes=48 * 1024 * 1024),
        )(bit_order, gate_block, amplitudes[0], chosen)

    placed = (P("wide", None, "narrow"), P(None, "wide", "narrow"), P(), P(), P())
    return jax.shard_map(
        per_device, mesh=mesh, in_specs=placed, out_specs=P(None, "wide", "narrow"), check_vma=False
    )
```

```python
import functools

import jax
import jax.numpy as jnp
from jax import lax
from jax.experimental import pallas as pl
from jax.experimental.pallas import tpu as pltpu
from jax.sharding import PartitionSpec as P

F32 = jnp.float32
BF16 = jnp.bfloat16
MESH = pl.DeviceIdType.MESH


def slice_kernel(bits_ref, partner_ref, chosen_ref, sem):
    number = bits_ref[0]
    for j in range(1, bits_ref.shape[0]):
        number = number + bits_ref[j] * (1 << j)
    copy = pltpu.make_async_copy(partner_ref.at[number], chosen_ref, sem)
    copy.start()
    copy.wait()


def choose(partner, slice_bits):
    _, rows, cols = partner.shape
    return pl.pallas_call(
        slice_kernel,
        out_shape=pltpu.VMEM((rows, cols), F32),
        in_specs=[pl.BlockSpec(memory_space=pltpu.SMEM), pl.BlockSpec(memory_space=pl.ANY)],
        out_specs=pl.BlockSpec(memory_space=pltpu.VMEM),
        scratch_shapes=[pltpu.SemaphoreType.DMA],
    )(slice_bits, partner)


def split2(x):
    hi = x.astype(BF16)
    return hi, (x - hi.astype(F32)).astype(BF16)


def dot_nt(a, b):
    return lax.dot_general(a, b, (((1,), (1,)), ((), ())), preferred_element_type=F32)


HALVES = 4

ORDERS = {
    (0, 0, 0): ('BBBBBBBBTTTTThaTTTsssaaaaaampqrn', '1246357', '321'),
    (0, 0, 1): ('IIIIIIIIBBThBBTaBBTBTBsssaTaTaTaaTampqrn', '1465723', '321'),
    (0, 1, 0): ('aIIIBIBhBIBIBIIBsssBaBaaaaampqrn', '1426357', '321'),
    (0, 1, 1): ('TTTTTTTaTIhIIBIBsssIBaBaIBIaaaBIamBpqBrn', '1465723', '321'),
    (1, 0, 0): ('ITITITITITITITITBBhBBaBBBBsssaaaaaampqrn', '3046175', '302'),
    (1, 0, 1): ('BBBBBBBBTTTTThTTaTsssaaaaaampqrn', '3046157', '302'),
    (1, 1, 0): ('ITITITITIBTITBaIBTITBBBBBhsssaaaaaampqrn', '3046157', '302'),
    (1, 1, 1): ('aIIIIIBIhBIBIBBBBBsssaaaaaampqrn', '3064175', '302'),
}


def tables():
    orders, row_words, stage_words = [], [], []
    for z in range(4):
        for x in range(2):
            for c in range(2):
                flip = z >= 2
                order, rows, stages = ORDERS[(3 - z, 1 - x, 1 - c) if flip else (z, x, c)]
                rows = [(3 - int(r) // 2) * 2 + int(r) % 2 if flip else int(r) for r in rows]
                stages = [3 - int(r) if flip else int(r) for r in stages]
                orders.append([" ITBashmnpqr".index(e) for e in order])
                row_words.append(sum(r * 8 ** k for k, r in enumerate(rows)))
                stage_words.append(sum(r * 4 ** k for k, r in enumerate(stages)))
    length = -(-max(len(o) for o in orders) // 7)
    words = [[sum(e * 16 ** k for k, e in enumerate(o[w * 7:w * 7 + 7])) for o in orders] for w in range(length)]
    return words, row_words, stage_words


def kernel(wides, order_ref, gate_ref, amp_ref, chosen_ref, out_ref,
           send_a, staged, rows_in, mixed, mixed_in, mix_hi, mix_lo, held,
           own_sem, z_send, side_send, y_send, first_send, held_recv,
           a_send, a_recv, st_send, st_recv, sf_send, ax_send, ax_recv, m_send, m_recv, near_sem):
    me = lax.axis_index("wide")
    nar = lax.axis_index("narrow")
    lines = wides // 2
    zs_per = lines // 4
    z, y = me // 2, me % 2
    x, c = nar // 2, nar % 2
    rows, cols = amp_ref.shape
    out_bits, low_rows, wide_cols = out_ref.shape
    block = held.shape[2]
    half = block // HALVES
    flat = out_bits * low_rows

    def dev(zz, yy, xx, cc):
        return (zz * 2 + yy, xx * 2 + cc)

    core_peer = dev(z, y, x, 1 - c)

    def rc(src, dst, ssem, rsem, device):
        return pltpu.make_async_remote_copy(
            src_ref=src, dst_ref=dst, send_sem=ssem, recv_sem=rsem,
            device_id=device, device_id_type=MESH)

    barrier = pltpu.get_barrier_semaphore()

    def greet(device):
        pl.semaphore_signal(barrier, inc=1, device_id=device, device_id_type=MESH)

    def near_z(do):
        pl.when(z > 0)(lambda: do(z - 1))
        pl.when(z < lines - 1)(lambda: do(z + 1))

    greet(core_peer)
    for cc in range(2):
        greet(dev(z, 1 - y, x, cc))
        greet(dev(z, y, 1 - x, cc))
        near_z(lambda zz: greet(dev(zz, y, x, cc)))

    row_ids = lax.broadcasted_iota(jnp.int32, (rows, 128), 0)
    source = jnp.zeros((rows, 128), jnp.int32)
    for j in range(order_ref.shape[0]):
        source = source + (lax.shift_right_logical(row_ids, jnp.broadcast_to(order_ref[j], row_ids.shape)) & 1) * (1 << j)
    lane = lax.broadcasted_iota(jnp.int32, (rows, 128), 1)
    onehot = jnp.concatenate(
        [jnp.where(lane + t * 128 == source, 1.0, 0.0).astype(BF16) for t in range(rows // 128)], axis=1)
    amp = amp_ref[...]
    a1 = amp.astype(BF16)
    rest = amp - a1.astype(F32)
    a2 = rest.astype(BF16)
    a3 = (rest - a2.astype(F32)).astype(BF16)
    moved = (jnp.dot(onehot, a3, preferred_element_type=F32)
             + jnp.dot(onehot, a2, preferred_element_type=F32)
             + jnp.dot(onehot, a1, preferred_element_type=F32))
    send_a[...] = moved.reshape(send_a.shape)

    ends = jnp.where(z > 0, 1, 0) + jnp.where(z < lines - 1, 1, 0)
    pl.semaphore_wait(barrier, 5 + 2 * ends)

    quarter0 = z // zs_per
    x0, c0 = quarter0 // 2, quarter0 % 2
    j0 = (z % zs_per) * 2 + y
    cross0 = (x0 + x) % 2
    slot0 = (1 - cross0) * (2 * x) + cross0 * 4 + c

    def part(p):
        return pl.ds(p * half, half)

    def own(way, device, slot, p):
        return rc(chosen_ref.at[part(p)], held.at[slot, j0, part(p)], first_send.at[way, p], held_recv.at[slot, j0, p], device)

    def own_up(p):
        return own(0, dev((z + 1) % lines, y, x, c0), slot0, p)

    def own_down(p):
        return own(1, dev((z + lines - 1) % lines, y, x, c0), slot0, p)

    def own_side(p):
        return own(2, dev(z, (y + 1 - cross0) % 2, (x + cross0) % 2, c0), x * 2 + c, p)

    def own_core(p):
        return own(3, core_peer, x * 2 + c, p)

    own_copy = pltpu.make_async_copy(chosen_ref, held.at[x * 2 + c, j0], own_sem)
    here = cross0 == 0
    rows_in[x, me] = send_a[me]

    def a_out(zz, yy):
        to = zz * 2 + yy
        return rc(send_a.at[to], rows_in.at[x, me], a_send.at[to], a_recv.at[me], (to, nar))

    def a_in(frm):
        return rc(send_a.at[frm], rows_in.at[x, frm], a_send.at[frm], a_recv.at[frm], (frm, nar))

    def stage(zz):
        return rc(send_a.at[zz * 2 + 1 - y], staged.at[zz], st_send.at[zz], st_recv.at[zz], dev(z, 1 - y, x, c))

    def stage_on(zz):
        frm = z * 2 + 1 - y
        return rc(staged.at[zz], rows_in.at[x, frm], sf_send.at[zz], a_recv.at[frm], dev(zz, y, x, c))

    def ax_out(h):
        return rc(rows_in.at[x, h], rows_in.at[x, h], ax_send.at[h], ax_recv.at[h], dev(z, y, 1 - x, c))

    def ax_in(h):
        return rc(rows_in.at[1 - x, h], rows_in.at[1 - x, h], ax_send.at[h], ax_recv.at[h], dev(z, y, 1 - x, c))

    def line(d, do):
        pl.when(z - d >= 0)(lambda: do(z - d))
        pl.when(z + d < lines)(lambda: do(z + d))

    def each_line(do):
        if lines == 4:
            for d in range(lines - 1, 0, -1):
                line(d, do)
        else:
            @pl.loop(1, lines)
            def _(d):
                line(d, do)

    def send_stage():
        each_line(lambda zz: stage(zz).start())
        a_out(z, 1 - y).start()

    pl.when(cross0 == 1)(send_stage)
    for p in range(HALVES):
        pl.when(z < lines - 1)(lambda: own_up(p).start())
        pl.when(z > 0)(lambda: own_down(p).start())
        own_side(p).start()
    pl.when(here)(send_stage)
    ax_out(me).start()

    @pl.when(here & (c0 != c))
    def _():
        for p in range(HALVES):
            own_core(p).start()

    @pl.when(here & (c0 == c))
    def _():
        own_copy.start()

    def tell(r):
        near_z(lambda zz: pl.semaphore_signal(
            near_sem.at[r - 2], inc=1, device_id=dev(zz, y, x, c), device_id_type=MESH))

    def heard(r):
        pl.semaphore_wait(near_sem.at[r - 2], ends)

    def forward_stage():
        def one(zz):
            stage(zz).wait_recv()
            stage_on(zz).start()
        each_line(one)

    def pass_one(zz, yy):
        h = zz * 2 + yy
        a_in(h).wait_recv()
        ax_out(h).start()

    def pass_rows(d):
        line(d, lambda zz: pass_one(zz, y))
        line(d, lambda zz: pass_one(zz, 1 - y))

    def travel(zb, cb, p, to_z):
        q = zb // zs_per
        cross = (q // 2 + x) % 2
        i = zb % zs_per
        slot = (1 - cross) * (2 * x) + cross * 4 + cb
        src = held.at[slot, i * 2 + y, part(p)]
        on = rc(src, src, z_send.at[slot, i, p], held_recv.at[slot, i * 2 + y, p], dev(to_z % lines, y, x, c))
        side = rc(src, held.at[x * 2 + cb, i * 2 + y, part(p)], side_send.at[slot, i, p],
                  held_recv.at[x * 2 + cb, i * 2 + y, p],
                  dev(z, (y + 1 - cross) % 2, (x + cross) % 2, c))
        return on, side

    def take(zb, cb, p, to_z, more):
        on, side = travel(zb, cb, p, to_z)
        on.wait_recv()
        pl.when(more)(lambda: on.start())
        side.start()

    def line_step(d):
        def go(zb, to_z, more):
            for p in range(HALVES):
                for cb in range(2):
                    take(zb, cb, p, to_z, more)
        pl.when((z - d >= 0) & (((z - d + lines) // zs_per) % 2 == c))(lambda: go(z - d, z + 1, z < lines - 1))
        pl.when((z + d < lines) & (((z + d) // zs_per) % 2 == c))(lambda: go(z + d, z - 1 + lines, z > 0))

    def over_y(zb, cb, p):
        i = zb % zs_per
        slot = (1 - x) * 2 + cb
        src = held.at[slot, i * 2 + y, part(p)]
        return rc(src, src, y_send.at[i, cb, p], held_recv.at[slot, i * 2 + y, p], dev(z, 1 - y, x, c))

    def take_x(zb, cb, p):
        copy = over_y(zb, cb, p)
        copy.wait_recv()
        copy.start()

    def x_step(d):
        def go(zb):
            for p in range(HALVES):
                for cb in range(2):
                    take_x(zb, cb, p)
        pl.when((z - d >= 0) & ((z - d + lines) // zs_per == nar + 4))(lambda: go(z - d))
        if not (isinstance(d, int) and d == 0):
            pl.when((z + d < lines) & ((z + d) // zs_per == nar))(lambda: go(z + d))

    def mix(xb):
        @pl.loop(0, out_bits)
        def _(q):
            acc = gate_ref[q, 0] * rows_in[xb, 0]
            for h in range(1, wides):
                acc = acc + gate_ref[q, h] * rows_in[xb, h]
            mixed[xb, pl.ds(pl.multiple_of(q * low_rows, 8), low_rows)] = acc

    def to_core(xb):
        return rc(mixed.at[xb], mixed_in.at[xb], m_send.at[xb], m_recv.at[xb], core_peer)

    def keep(xb, cc, value):
        hi, lo = split2(value)
        mix_hi[xb * 2 + cc] = hi
        mix_lo[xb * 2 + cc] = lo

    def arrived(slot, yb, i):
        for p in range(HALVES):
            src = held.at[slot, i * 2 + yb, part(p)]
            rc(src, src, y_send.at[i, 0, p], held_recv.at[slot, i * 2 + yb, p], core_peer).wait_recv()

    def both(slots, b):
        left, right = [], []
        for slot, value in zip(slots, b):
            bh, bl = split2(value)
            mh, ml = mix_hi[slot], mix_lo[slot]
            left += [mh, ml, mh]
            right += [bl, bh, bh]
        return dot_nt(jnp.concatenate(left, axis=1), jnp.concatenate(right, axis=1))

    def put(at_n, value, first):
        value = value.reshape(out_bits, low_rows, value.shape[1])
        if first:
            out_ref[:, :, at_n] = value
        else:
            out_ref[:, :, at_n] = out_ref[:, :, at_n] + value

    def add(slots, yb, first=False):
        if zs_per == 1:
            at_n = pl.ds(pl.multiple_of(yb * block, 128), block)
            put(at_n, both(slots, [held[slot, yb] for slot in slots]), first)
        else:
            put(slice(None), both(slots, [held[slot].reshape(wide_cols, cols) for slot in slots]), first)

    def add_two(xb, yb, first=False):
        if isinstance(first, bool) and first:
            last_own(yb)
        slots = [xb * 2, xb * 2 + 1]
        if yb is not y:
            for slot in slots:
                arrived(slot, yb, 0)
        add(slots, yb, first)

    def last_own(yb):
        if yb is y:
            @pl.when(here & (c0 == c))
            def _():
                own_copy.wait()
                arrived(x * 2 + 1 - c, y, z % zs_per)

    def others(i, slots):
        for xb in slots:
            for cb in range(2):
                arrived(xb * 2 + cb, 1 - y, i)

    def mix_near():
        mix(x)
        to_core(x).start()
        keep(x, c, mixed[x])

    def swap_near():
        to_core(x).wait_recv()
        keep(x, 1 - c, mixed_in[x])

    def mix_far():
        ax_in(me).wait_recv()

        @pl.loop(1, wides)
        def _(s):
            ax_in((me + s) % wides).wait_recv()
        mix(1 - x)
        to_core(1 - x).start()
        keep(1 - x, c, mixed[1 - x])

    tell(2)
    heard(2)
    if lines == 4:
        tell(3)
        place = z * 4 + x * 2 + c
        words, rows_word, stage_word = tables()

        def pick(values):
            if len(set(values)) == 1:
                return jnp.int32(values[0])
            word = jnp.int32(values[0])
            for k in range(1, len(values)):
                word = jnp.where(place == k, values[k], word)
            return word

        steps = [pick(v) for v in words]
        other = (1 - x) * 2 + c

        def passing(zb, n):
            below = zb < z
            take(zb, n % 2, n // 2, jnp.where(below, z + 1, z + 3), jnp.where(below, z < lines - 1, z > 0))

        def event(_, carry):
            word, ni, nt, nb, a_word, s_word = carry
            kind = word % 16

            @pl.when(kind < 4)
            def _():
                @pl.when(kind == 1)
                def _():
                    passing(nar, ni)

                @pl.when(kind == 2)
                def _():
                    passing(other, nt)

                @pl.when(kind == 3)
                def _():
                    take_x(nar, nb % 2, nb // 2)

            @pl.when((kind >= 4) & (kind < 7))
            def _():
                @pl.when(kind == 4)
                def _():
                    pass_one(a_word % 8 // 2, (y + a_word) % 2)

                @pl.when(kind == 5)
                def _():
                    zz = s_word % 4
                    stage(zz).wait_recv()
                    stage_on(zz).start()

                @pl.when(kind == 6)
                def _():
                    heard(3)
                    each_line(lambda zz: a_out(zz, y).start())

            @pl.when(kind >= 7)
            def _():
                pl.when(kind == 7)(mix_near)
                pl.when(kind == 8)(mix_far)
                pl.when(kind == 9)(swap_near)
                pl.when(kind == 10)(lambda: add_two(x, y, True))
                pl.when(kind == 11)(lambda: add_two(x, 1 - y, True))
            one = lambda k: jnp.where(kind == k, 1, 0)
            return (word // 16, ni + one(1), nt + one(2), nb + one(3),
                    jnp.where(kind == 4, a_word // 8, a_word), jnp.where(kind == 5, s_word // 4, s_word))

        def stretch(w, carry):
            word = steps[0]
            for k in range(1, len(steps)):
                word = jnp.where(w == k, steps[k], word)
            return lax.fori_loop(0, 7, event, (word, *carry))[1:]

        zero = jnp.int32(0)
        lax.fori_loop(0, len(steps), stretch, (zero, zero, zero, pick(rows_word), pick(stage_word)))
    else:
        @pl.loop(3, lines)
        def _(r):
            tell(r)
            heard(r)

        x_step(0)
        each_line(lambda zz: a_out(zz, y).start())
        forward_stage()

        @pl.loop(1, lines)
        def _(d):
            line_step(d)
            x_step(d)
        pass_one(z, 1 - y)

        @pl.loop(1, lines)
        def _(d):
            pass_rows(d)
        mix_near()
        mix_far()
        swap_near()
    def settle():
        to_core(x).wait_send()

        @pl.loop(0, wides)
        def _(h):
            ax_out(h).wait_send()

        a_out(z, 1 - y).wait_send()

        @pl.loop(1, lines)
        def _(s):
            zz = (z + s) % lines
            a_out(zz, y).wait_send()
            stage(zz).wait_send()
            stage_on(zz).wait_send()
        for p in range(HALVES):
            pl.when(z < lines - 1)(lambda: own_up(p).wait_send())
            pl.when(z > 0)(lambda: own_down(p).wait_send())
            own_side(p).wait_send()
            pl.when(here & (c0 != c))(lambda: own_core(p).wait_send())

        def sent(d):
            def go(zb, more):
                for p in range(HALVES):
                    for cb in range(2):
                        on, side = travel(zb, cb, p, z)
                        pl.when(more)(lambda: on.wait_send())
                        side.wait_send()
            pl.when((z - d >= 0) & (((z - d + lines) // zs_per) % 2 == c))(lambda: go(z - d, z < lines - 1))
            pl.when((z + d < lines) & (((z + d) // zs_per) % 2 == c))(lambda: go(z + d, z > 0))

        @pl.loop(1, lines)
        def _(d):
            sent(d)

    mine, theirs = (1 - x) * 2 + c, (1 - x) * 2 + 1 - c
    if zs_per == 1:
        add([mine], y)
        arrived(mine, 1 - y, 0)
        add([mine], 1 - y)
        to_core(1 - x).wait_recv()
        keep(1 - x, 1 - c, mixed_in[1 - x])
        add([theirs], y)
        settle()
        arrived(theirs, 1 - y, 0)
        add([theirs], 1 - y)
    else:
        to_core(1 - x).wait_recv()
        keep(1 - x, 1 - c, mixed_in[1 - x])
        last_own(y)
        for xb in (x, 1 - x):
            @pl.loop(0, zs_per)
            def _(i):
                others(i, (xb,))
            add([xb * 2, xb * 2 + 1], 0, xb is x)
        settle()

    to_core(1 - x).wait_send()

    @pl.loop(0, zs_per)
    def _(i):
        for p in range(HALVES):
            for cb in range(2):
                over_y(nar * zs_per + i, cb, p).wait_send()


def solution(mesh):
    wides = mesh.shape["wide"]

    def per_device(amplitudes, partner, gate_block, slice_bits, bit_order):
        chosen = choose(partner, slice_bits)
        rows, cols = amplitudes.shape[1:]
        out_bits = gate_block.shape[0]
        low_rows = rows // wides
        block = chosen.shape[0]
        own = block * wides // mesh.shape["narrow"]
        flat = out_bits * low_rows
        smem = pl.BlockSpec(memory_space=pltpu.SMEM)
        vmem = pl.BlockSpec(memory_space=pltpu.VMEM)
        dma = pltpu.SemaphoreType.DMA
        lines = wides // 2
        zs_per = lines // 4
        return pl.pallas_call(
            functools.partial(kernel, wides),
            out_shape=jax.ShapeDtypeStruct((out_bits, low_rows, own), F32),
            in_specs=[smem, smem, vmem, vmem],
            out_specs=vmem,
            scratch_shapes=[
                pltpu.VMEM((wides, low_rows, cols), F32),
                pltpu.VMEM((lines, low_rows, cols), F32),
                pltpu.VMEM((2, wides, low_rows, cols), F32),
                pltpu.VMEM((2, flat, cols), F32),
                pltpu.VMEM((2, flat, cols), F32),
                pltpu.VMEM((4, flat, cols), BF16),
                pltpu.VMEM((4, flat, cols), BF16),
                pltpu.VMEM((6, zs_per * 2, block, cols), F32),
                dma,
                dma((6, zs_per, HALVES)), dma((6, zs_per, HALVES)), dma((zs_per, 2, HALVES)),
                dma((4, HALVES)), dma((6, zs_per * 2, HALVES)),
                dma((wides,)), dma((wides,)), dma((lines,)), dma((lines,)), dma((lines,)), dma((wides,)), dma((wides,)),
                dma((2,)), dma((2,)),
                pltpu.SemaphoreType.REGULAR((lines,)),
            ],
            compiler_params=pltpu.CompilerParams(
                collective_id=0, has_side_effects=True, vmem_limit_bytes=48 * 1024 * 1024),
        )(bit_order, gate_block, amplitudes[0], chosen)

    placed = (P("wide", None, "narrow"), P(None, "wide", "narrow"), P(), P(), P())
    return jax.shard_map(
        per_device, mesh=mesh, in_specs=placed, out_specs=P(None, "wide", "narrow"), check_vma=False
    )
```
